32 devices in a mesh: dp: 4 (over z), fsdp: 8 (over y, x, core).
Axes of the slice: x: 2, y: 2, z: 4, core: 2. Of those that a mesh axis runs over, the one named last changes fastest.
Arguments:
- tokens: bfloat16 [2, 32, 128, 2048], P(None, ('dp', 'fsdp')), may hold values from -6 to 6
- lengths: int32 [2, 32], replicated, may hold values from 1 to 128, 2560 in all within a row
- order: int32 [2, 32], replicated, may hold values from 0 to 31, as said below
- w_query: bfloat16 [2048, 2048], P(('dp', 'fsdp')), may hold values from -0.125 to 0.125
- w_key: bfloat16 [2048, 2048], P(('dp', 'fsdp')), may hold values from -0.125 to 0.125
- w_value: bfloat16 [2048, 2048], P(('dp', 'fsdp')), may hold values from -0.125 to 0.125
- w_output: bfloat16 [2048, 2048], P(('dp', 'fsdp')), may hold values from -1 to 1
- w_gate: bfloat16 [2048, 8192], P(('dp', 'fsdp')), may hold values from -0.125 to 0.125
- w_up: bfloat16 [2048, 8192], P(('dp', 'fsdp')), may hold values from -0.125 to 0.125
- w_down: bfloat16 [2048, 8192], P(('dp', 'fsdp')), may hold values from -0.0625 to 0.0625
- gain_attn: bfloat16 [2048], P(('dp', 'fsdp')), may hold values from 0.5 to 1.5
- gain_ffn: bfloat16 [2048], P(('dp', 'fsdp')), may hold values from 0.5 to 1.5
- cotangent: bfloat16 [2, 32, 128, 2048], P(None, ('dp', 'fsdp')), may hold values from -6 to 6
Outputs:
- output: bfloat16 [2, 32, 128, 2048], P(None, ('dp', 'fsdp'))
- grad_tokens: bfloat16 [2, 32, 128, 2048], P(None, ('dp', 'fsdp'))
- grad_w_query: float32 [2048, 2048], P(('dp', 'fsdp'))
- grad_w_key: float32 [2048, 2048], P(('dp', 'fsdp'))
- grad_w_value: float32 [2048, 2048], P(('dp', 'fsdp'))
- grad_w_output: float32 [2048, 2048], P(('dp', 'fsdp'))
- grad_w_gate: float32 [2048, 8192], P(('dp', 'fsdp'))
- grad_w_up: float32 [2048, 8192], P(('dp', 'fsdp'))
- grad_w_down: float32 [2048, 8192], P(('dp', 'fsdp'))
- grad_gain_attn: float32 [2048], P(('dp', 'fsdp'))
- grad_gain_ffn: float32 [2048], P(('dp', 'fsdp'))
The draws below stay inside these ranges and needn't reach their ends.
Inputs may be any that keep to these rules, and one draw needn't show every extreme that they name: `order`: for each micro-batch, a permutation of 0 to 31 that maps every aligned block of 8 sequences onto itself.
All inputs are finite; a program needn't handle non-finite values.
Results may differ from the reference program's by a relative error of at most 0.014.
Values may be sent and summed in bfloat16 or wider, within the bound.
No kernel may reach another device: no remote copies, remote signals or barrier semaphores. Data moves between devices by JAX's collectives and lax.ppermute only.
A program may use at most 512 MiB of HBM per device.

```python
import math
import jax
import jax.numpy as jnp
import numpy as np
from jax import lax

D = 2048
H = 16
HD = 128
FF = 8192
CAP = 128
MB = 2
SEQS_MB = 32
GROUP = 8
LIVE_TOTAL = 2560


def draw_order(key, part):
    block_total = SEQS_MB // GROUP
    keys_all = jax.random.split(key, MB * block_total)
    shuffled = jax.vmap(lambda one_key: jax.random.permutation(one_key, GROUP))(keys_all)
    offsets = jnp.arange(MB * block_total, dtype=jnp.int32) % block_total * GROUP
    return (shuffled.astype(jnp.int32) + offsets[:, None]).reshape(MB, SEQS_MB)


def raised(values, key, source, target, shards_of, factor):
    def block_of(dim):
        return (jnp.arange(values.shape[dim]) // (values.shape[dim] // shards_of)).reshape((-1,) + (1,) * (values.ndim - 1 - dim))

    first = jax.random.permutation(key, shards_of)[block_of(target)]
    second = (block_of(target) + shards_of // 2) % shards_of
    return jnp.where((block_of(source) == first) | (block_of(source) == second), factor * values, values)


def levels(rng, dims, pieces, low, largest):
    factor_of = 1.0
    for dim, parts in pieces:
        heights = jax.random.uniform(jax.random.fold_in(jax.random.fold_in(rng, 6), dim), (parts,), jnp.float32, low / len(pieces), largest / len(pieces))
        factor_of = factor_of * jnp.repeat(jnp.exp(heights), dims[dim] // parts).reshape((-1,) + (1,) * (len(dims) - 1 - dim))
    return factor_of


def length_profile(count, total, limit, lean):
    portions = [(1 << 20) // math.isqrt(standing ** lean) + 1 for standing in range(2, count + 1)]
    rest, counts = total - limit - (count - 1), [1] * (count - 1)
    while rest > 0:
        movable = [i for i in range(count - 1) if counts[i] < limit]
        pool, budget = sum([portions[i] for i in movable]), rest
        for i in movable:
            more = min(limit - counts[i], max(1, budget * portions[i] // pool), rest)
            counts[i] = counts[i] + more
            rest = rest - more
    return np.array([limit] + counts)


def ragged_sizes(key, number_of, total, most, skew):
    if number_of == 2:
        one = jax.random.randint(key, (), max(1, total - most), min(most, total - 1) + 1)
        return jnp.stack([one, total - one])
    tallies = jnp.asarray(length_profile(number_of, total, most, skew), jnp.int32)
    pairs = (number_of - 1) // 2
    giver, taker = tallies[1:1 + 2 * pairs:2], tallies[2:2 + 2 * pairs:2]
    slack = jnp.minimum(giver - 1, most - taker)
    shifted = jax.random.randint(jax.random.fold_in(key, 1), (pairs,), 0, 1 << 20) % (slack + 1)
    tallies = tallies.at[1:1 + 2 * pairs:2].set(giver - shifted).at[2:2 + 2 * pairs:2].set(taker + shifted)
    return tallies[jax.random.permutation(jax.random.fold_in(key, 2), number_of)]


def centred(rng, extent, deviation, reach, cuts=(), kind=jnp.bfloat16):
    array = jax.random.normal(rng, extent, jnp.float32) * deviation
    if len(cuts) > 0:
        array = levels(rng, extent, cuts, -0.22, 0.18) * array
    return jnp.clip(array, min=-reach, max=reach).astype(kind)


def noise_with(stream_key, shape, deviation, limit, cuts, heavy, kind=jnp.bfloat16):
    entries = deviation * jax.random.normal(stream_key, shape, jnp.float32)
    if cuts:
        entries = entries * levels(stream_key, shape, cuts, -0.22, 0.18)
    return jnp.clip(raised(entries, jax.random.fold_in(stream_key, 3), *heavy), -limit, limit).astype(kind)


def setup_inputs(seed: int = 0) -> dict:
    key_of = jax.random.split(jax.random.key(seed), 14)
    return {
        "tokens": centred(key_of[0], (MB, SEQS_MB, CAP, D), 1.0, 6.0, ((1, 32),)),
        "lengths": jax.vmap(lambda own: ragged_sizes(own, SEQS_MB, LIVE_TOTAL, CAP, 1))(jax.random.split(key_of[1], MB)).reshape((MB, SEQS_MB)).astype(jnp.int32),
        "order": draw_order(jax.random.fold_in(key_of[13], 71), 0),
        "w_query": centred(key_of[3], (D, D), D ** -0.5, 0.125, ((0, 32),)),
        "w_key": centred(key_of[4], (D, D), D ** -0.5, 0.125, ((0, 32),)),
        "w_value": centred(key_of[5], (D, D), D ** -0.5, 0.125, ((0, 32),)),
        "w_output": centred(key_of[6], (D, D), (D // 64) ** -0.5, 1.0, ((0, 32),)),
        "w_gate": centred(key_of[7], (D, FF), D ** -0.5, 0.125, ((0, 32),)),
        "w_up": centred(key_of[8], (D, FF), D ** -0.5, 0.125, ((0, 32),)),
        "w_down": centred(key_of[9], (D, FF), FF ** -0.5, 0.0625, ((0, 32),)),
        "gain_attn": jnp.clip(1.0 + 0.1 * jax.random.normal(key_of[10], (D,), jnp.float32), 0.5, 1.5).astype(jnp.bfloat16),
        "gain_ffn": jnp.clip(1.0 + 0.1 * jax.random.normal(key_of[11], (D,), jnp.float32), 0.5, 1.5).astype(jnp.bfloat16),
        "cotangent": noise_with(key_of[12], (MB, SEQS_MB, CAP, D), 1.0, 6.0, ((1, 32),), (1, 3, 32, 2.75)),
    }


@jax.custom_vjp
def low(v):
    return lax.optimization_barrier(v.astype(jnp.bfloat16)).astype(jnp.float32)

@jax.custom_vjp
def low_back(v):
    return v

def low_keep(v):
    return (low(v), None)

def low_pass(kept, grad):
    return (grad,)

def back_keep(v):
    return (v, None)

def back_low(kept, grad):
    return (low(grad),)
low.defvjp(low_keep, low_pass)
low_back.defvjp(back_keep, back_low)
epsilon = 1e-05
highest = lax.Precision.HIGHEST

def rope_tables():
    halfway = HD // 2
    position = jnp.arange(CAP, dtype=jnp.float32)
    inverse = 10000.0 ** (-2.0 * jnp.arange(halfway, dtype=jnp.float32) / HD)
    angles = position[:, None] * inverse[None, :]
    return (jnp.cos(angles)[:, None, :], jnp.sin(angles)[:, None, :])

def rotate(values, cosine, sine):
    halfway = values.shape[-1] // 2
    first_half = values[..., :halfway]
    second_half = values[..., halfway:]
    return jnp.concatenate([first_half * cosine - second_half * sine, second_half * cosine + first_half * sine], axis=-1)

def project(left, right):
    return jnp.einsum('gtd,de->gte', left, right, precision=highest)

def block_forward(params, block_x, block_mask):
    w_query, w_key, w_value, w_output, w_gate, w_up, w_down, gain_attn, gain_ffn = params
    blocks = block_x.shape[0]
    cosine, sine = rope_tables()
    inverse_one = lax.rsqrt(lax.optimization_barrier(jnp.mean(block_x * block_x, axis=-1, keepdims=True)) + epsilon)
    normed_one = low(block_x * inverse_one * gain_attn)
    raw_query = low_back(project(normed_one, w_query))
    raw_key = low_back(project(normed_one, w_key))
    values = low(low_back(project(normed_one, w_value))).reshape(blocks, CAP, H, HD)
    queries = low(rotate(raw_query.reshape(blocks, CAP, H, HD), cosine, sine))
    key_rows = low(rotate(raw_key.reshape(blocks, CAP, H, HD), cosine, sine))
    scores = jnp.einsum('gqhe,gkhe->ghqk', queries, key_rows, precision=highest) / math.sqrt(HD) - math.log(CAP)
    scores = low_back(scores)
    causal = (jnp.arange(CAP)[:, None] >= jnp.arange(CAP)[None, :]).astype(jnp.float32)
    allowed = causal[None, None, :, :] * block_mask[:, None, None, :]
    prob_rows = low(jax.nn.sigmoid(scores) * allowed)
    mixed_rows = jnp.einsum('ghqk,gkhe->gqhe', prob_rows, values, precision=highest).reshape(blocks, CAP, D)
    mixed_rows = low_back(low(mixed_rows))
    attended = low_back(project(mixed_rows, w_output))
    hidden_one = block_x + attended
    inverse_two = lax.rsqrt(lax.optimization_barrier(jnp.mean(hidden_one * hidden_one, axis=-1, keepdims=True)) + epsilon)
    normed_two = low(hidden_one * inverse_two * gain_ffn)
    gate_rows = low_back(project(normed_two, w_gate))
    up_rows = low_back(project(normed_two, w_up))
    activated = low(jax.nn.silu(gate_rows) * up_rows)
    returned = low_back(jnp.einsum('gtf,df->gtd', activated, w_down, precision=highest))
    return (hidden_one + returned) * block_mask[:, :, None]

def reference(tokens, lengths, order, w_query, w_key, w_value, w_output, w_gate, w_up, w_down, gain_attn, gain_ffn, cotangent):
    slot_ids = jnp.arange(SEQS_MB, dtype=jnp.int32)
    live = lax.optimization_barrier(jnp.sum(jnp.where(order[:, :, None] == slot_ids[None, None, :], lengths[:, None, :], 0), axis=-1))
    positions = jnp.arange(CAP, dtype=jnp.int32)
    masks = (positions[None, None, :] < live[:, :, None]).astype(jnp.float32)
    group_rows = math.gcd(SEQS_MB, max(1, 4096 // CAP))
    block_count = MB * SEQS_MB // group_rows
    masks = masks.reshape(block_count, group_rows, CAP)
    inputs = tokens.astype(jnp.float32).reshape(block_count, group_rows, CAP, D)
    params = tuple((matrix.astype(jnp.float32) for matrix in (w_query, w_key, w_value, w_output, w_gate, w_up, w_down, gain_attn, gain_ffn)))

    def forward(weights, block_inputs):

        def scan_step(unused, block_pair):
            return (unused, jax.checkpoint(block_forward)(weights, block_pair[0], block_pair[1]))
        _, outputs = lax.scan(scan_step, jnp.zeros((), jnp.float32), (block_inputs, masks))
        return outputs
    outputs, pullback = jax.vjp(forward, params, inputs)
    grad_params, grad_inputs = pullback(cotangent.astype(jnp.float32).reshape(block_count, group_rows, CAP, D))
    shape_full = (MB, SEQS_MB, CAP, D)
    return (outputs.reshape(shape_full).astype(jnp.bfloat16), grad_inputs.reshape(shape_full).astype(jnp.bfloat16), grad_params[0], grad_params[1], grad_params[2], grad_params[3], grad_params[4], grad_params[5], grad_params[6], grad_params[7], grad_params[8])
```

```python
import math

import jax
import jax.numpy as jnp
from jax import lax
from jax.sharding import PartitionSpec as P

H = 16
HD = 128
EPSILON = 1e-05
F32 = jnp.float32
BF16 = jnp.bfloat16


def rope_tables(length_cap, head_size):
    halfway = head_size // 2
    position = jnp.arange(length_cap, dtype=F32)
    inverse = 10000.0 ** (-2.0 * jnp.arange(halfway, dtype=F32) / head_size)
    angles = position[:, None] * inverse[None, :]
    return jnp.cos(angles)[:, None, :], jnp.sin(angles)[:, None, :]


def rotate(values, cosine, sine):
    halfway = values.shape[-1] // 2
    first_half = values[..., :halfway]
    second_half = values[..., halfway:]
    return jnp.concatenate(
        [first_half * cosine - second_half * sine, second_half * cosine + first_half * sine],
        axis=-1,
    )


def dot_nn(left, right):
    return lax.dot_general(left, right, (((1,), (0,)), ((), ())), preferred_element_type=F32)


def dot_nt(left, right):
    return lax.dot_general(left, right, (((1,), (1,)), ((), ())), preferred_element_type=F32)


def dot_tn(left, right):
    return lax.dot_general(left, right, (((0,), (0,)), ((), ())), preferred_element_type=F32)


def swap(value, offset):
    return lax.ppermute(value, "fsdp", [(i, i ^ offset) for i in range(8)])


def add_low(left, right):
    return (left.astype(F32) + right.astype(F32)).astype(BF16)


def gather_group(rows):
    if lax.axis_size("fsdp") != 8:
        return lax.all_gather(rows, "fsdp", axis=1)
    a, b = {0: rows[0]}, {0: rows[1]}
    a[2], b[4] = swap(a[0], 2), swap(b[0], 4)
    a[1], b[1] = swap(a[0], 1), swap(b[0], 1)
    a[4], b[2] = swap(a[0], 4), swap(b[0], 2)
    a[6], b[6] = swap(a[2], 4), swap(b[4], 2)
    a[3], b[5] = swap(a[2], 1), swap(b[4], 1)
    a[5], b[3] = swap(a[4], 1), swap(b[2], 1)
    a[7], b[7] = swap(a[6], 1), swap(b[6], 1)
    return jnp.stack([a[k] for k in range(8)] + [b[k] for k in range(8)]).reshape(
        (2, 8) + rows.shape[1:]
    )


def scatter_group(parts):
    if lax.axis_size("fsdp") != 8:
        return lax.psum_scatter(parts, "fsdp", scatter_dimension=1).astype(F32)
    pairs = parts.reshape((2, 4, 2) + parts.shape[2:])
    pairs = add_low(pairs[:, :, 0], swap(pairs[:, :, 1], 1))
    a, b = pairs[0], pairs[1]
    a = add_low(a[:2], swap(a[2:], 4))
    b = b.reshape((2, 2) + b.shape[1:])
    b = add_low(b[:, 0], swap(b[:, 1], 2))
    a = a[0].astype(F32) + swap(a[1], 2).astype(F32)
    b = b[0].astype(F32) + swap(b[1], 4).astype(F32)
    return jnp.stack([a, b])


def spread(pieces):
    count, rows, columns = pieces.shape
    return lax.all_to_all(pieces.reshape(count * rows, columns), "fsdp", 0, 0, tiled=True)


def per_device(
    tokens,
    lengths,
    order,
    w_query,
    w_key,
    w_value,
    w_output,
    w_gate,
    w_up,
    w_down,
    gain_attn,
    gain_ffn,
    cotangent,
):
    groups, members = lax.axis_size("dp"), lax.axis_size("fsdp")
    plane, member = lax.axis_index("dp"), lax.axis_index("fsdp")
    micro, _, cap, width = tokens.shape
    own_rows = w_query.shape[0]
    hidden = w_gate.shape[1]
    share = hidden // members
    sharers = HD // own_rows
    kinds = members // sharers
    my_heads = groups // sharers
    head_cols = my_heads * HD
    total = micro * members * cap
    scale = 1.0 / math.sqrt(HD)
    shift = -math.log(cap)

    slots = jnp.arange(order.shape[1], dtype=jnp.int32)
    block = jnp.arange(members, dtype=jnp.int32)
    at = plane * members + (block ^ member if members == 8 else block)
    chosen = jnp.sum(jnp.where(at[None, :, None] == slots, order[:, None, :], 0), axis=-1)
    live = jnp.sum(jnp.where(chosen[:, :, None] == slots, lengths[:, None, :], 0), axis=-1)
    position = jnp.arange(cap, dtype=jnp.int32)
    at_me = plane * members + member
    my_slot = jnp.sum(jnp.where(slots == at_me, order, 0), axis=-1)
    my_live = jnp.sum(jnp.where(slots == my_slot[:, None], lengths, 0), axis=-1)
    my_mask = (position < my_live[:, None]).astype(F32)[:, :, None]

    gain_one = gain_attn.astype(F32)[:, None]
    gain_two = gain_ffn.astype(F32)[:, None]

    def scaled(weight, gain):
        return (weight.astype(F32) * gain).astype(BF16)

    def by_head(weight):
        cut = weight.reshape(own_rows, sharers, my_heads, kinds, HD)
        return cut.transpose(3, 1, 0, 2, 4).reshape(members, own_rows, head_cols)

    def by_unit(weight):
        return weight.reshape(own_rows, members, share).transpose(1, 0, 2)

    def planes(value):
        return lax.all_gather(value, "dp", axis=0, tiled=True)

    wqkv = planes(
        spread(
            jnp.concatenate(
                [by_head(scaled(w, gain_one)) for w in (w_query, w_key, w_value)], axis=2
            )
        )
    )
    wgu = planes(
        spread(jnp.concatenate([by_unit(scaled(w, gain_two)) for w in (w_gate, w_up)], axis=2))
    )
    wd = planes(spread(by_unit(w_down)))
    raw = planes(w_output).reshape(sharers, my_heads, own_rows, width)
    subgroups = [[s * sharers + i for i in range(sharers)] for s in range(kinds)]

    def exchange(value):
        return lax.all_to_all(value, "fsdp", 0, 0, axis_index_groups=subgroups)

    wo = exchange(raw).transpose(1, 0, 2, 3).reshape(head_cols, width)

    x = tokens[:, 0].astype(F32)
    inverse_one = lax.rsqrt(jnp.mean(x * x, axis=-1, keepdims=True) + EPSILON)
    normal_one = x * inverse_one
    n1 = gather_group(normal_one.astype(BF16)).reshape(total, width)
    upstream = cotangent[:, 0].astype(F32) * my_mask
    returned_grad = gather_group(upstream.astype(BF16)).reshape(total, width)

    cosine, sine = rope_tables(cap, HD)
    causal = position[:, None] >= position[None, :]
    allowed = (
        causal[None, None] & (position[None, :] < live.reshape(-1, 1))[:, None, None, :]
    ).astype(F32)
    heads = (micro * members, cap, 3, my_heads, HD)
    qkv = dot_nn(n1, wqkv).reshape(heads)
    queries = rotate(qkv[:, :, 0], cosine, sine).astype(BF16)
    keys = rotate(qkv[:, :, 1], cosine, sine).astype(BF16)
    values = qkv[:, :, 2].astype(BF16)
    logits = (
        jnp.einsum("gqhe,gkhe->ghqk", queries, keys, preferred_element_type=F32) * scale + shift
    )
    gates = jax.nn.sigmoid(logits)
    probs = (gates * allowed).astype(BF16)
    mixed = (
        jnp.einsum("ghqk,gkhe->gqhe", probs, values, preferred_element_type=F32)
        .reshape(total, head_cols)
        .astype(BF16)
    )
    block_shape = (micro, members, cap, width)
    attended = scatter_group(dot_nn(mixed, wo).astype(BF16).reshape(block_shape))
    hidden_one = x + attended

    inverse_two = lax.rsqrt(jnp.mean(hidden_one * hidden_one, axis=-1, keepdims=True) + EPSILON)
    normal_two = hidden_one * inverse_two
    n2 = gather_group(normal_two.astype(BF16)).reshape(total, width)
    gate_up = dot_nn(n2, wgu)
    gate, up = gate_up[:, :share], gate_up[:, share:]
    sigmoid_gate = jax.nn.sigmoid(gate)
    swish = gate * sigmoid_gate
    activated = (swish * up).astype(BF16)
    returned = scatter_group(dot_nt(activated, wd).astype(BF16).reshape(block_shape))
    output = ((hidden_one + returned) * my_mask).astype(BF16)

    grad_activated = dot_nn(returned_grad, wd)
    grad_gate = grad_activated * up * (sigmoid_gate * (1.0 + gate * (1.0 - sigmoid_gate)))
    grad_up = grad_activated * swish
    grad_gu = jnp.concatenate([grad_gate.astype(BF16), grad_up.astype(BF16)], axis=1)
    back_two = scatter_group(dot_nt(grad_gu, wgu).astype(BF16).reshape(block_shape))
    grad_hidden = upstream + inverse_two * (
        back_two - normal_two * jnp.mean(back_two * normal_two, axis=-1, keepdims=True)
    )

    grad_attended = gather_group(grad_hidden.astype(BF16)).reshape(total, width)
    grad_mixed = (
        dot_nt(grad_attended, wo).astype(BF16).reshape(micro * members, cap, my_heads, HD)
    )
    grad_probs = jnp.einsum("gqhe,gkhe->ghqk", grad_mixed, values, preferred_element_type=F32)
    grad_logits = (grad_probs * gates * (1.0 - gates) * allowed).astype(BF16)
    grad_values = jnp.einsum("ghqk,gqhe->gkhe", probs, grad_mixed, preferred_element_type=F32)
    turned_q = (
        jnp.einsum("ghqk,gkhe->gqhe", grad_logits, keys, preferred_element_type=F32) * scale
    )
    turned_k = (
        jnp.einsum("ghqk,gqhe->gkhe", grad_logits, queries, preferred_element_type=F32) * scale
    )
    grad_qkv = jnp.concatenate(
        [
            value.reshape(total, head_cols).astype(BF16)
            for value in (
                rotate(turned_q, cosine, -sine),
                rotate(turned_k, cosine, -sine),
                grad_values,
            )
        ],
        axis=1,
    )
    back_one = scatter_group(dot_nt(grad_qkv, wqkv).astype(BF16).reshape(block_shape))
    grad_tokens = (
        grad_hidden
        + inverse_one
        * (back_one - normal_one * jnp.mean(back_one * normal_one, axis=-1, keepdims=True))
    ).astype(BF16)

    def home(value):
        mine = lax.psum_scatter(value.astype(BF16), "dp", scatter_dimension=0, tiled=True)
        return lax.all_to_all(mine, "fsdp", 0, 0, tiled=True).reshape(members, own_rows, -1)

    sum_d = home(dot_tn(returned_grad, activated))
    sum_gu = home(dot_tn(n2, grad_gu))
    sum_qkv = home(dot_tn(n1, grad_qkv))
    part_o = dot_tn(mixed, grad_attended).astype(BF16)
    part_o = exchange(part_o.reshape(my_heads, sharers, own_rows, width).transpose(1, 0, 2, 3))
    grad_wo = lax.psum_scatter(
        part_o.reshape(groups, own_rows, width), "dp", scatter_dimension=0
    ).astype(F32)

    def from_heads(value):
        cut = value.reshape(kinds, sharers, own_rows, my_heads, HD)
        return cut.transpose(2, 1, 3, 0, 4).reshape(own_rows, width).astype(F32)

    def from_units(value):
        return value.transpose(1, 0, 2).reshape(own_rows, hidden).astype(F32)

    raw_qkv = [
        from_heads(sum_qkv[:, :, i * head_cols : (i + 1) * head_cols]) for i in range(3)
    ]
    raw_gu = [from_units(sum_gu[:, :, i * share : (i + 1) * share]) for i in range(2)]
    grad_gain_one = sum(
        jnp.sum(g * w.astype(F32), axis=1)
        for g, w in zip(raw_qkv, (w_query, w_key, w_value), strict=True)
    )
    grad_gain_two = sum(
        jnp.sum(g * w.astype(F32), axis=1) for g, w in zip(raw_gu, (w_gate, w_up), strict=True)
    )
    return (
        output[:, None],
        grad_tokens[:, None],
        raw_qkv[0] * gain_one,
        raw_qkv[1] * gain_one,
        raw_qkv[2] * gain_one,
        grad_wo,
        raw_gu[0] * gain_two,
        raw_gu[1] * gain_two,
        from_units(sum_d),
        grad_gain_one,
        grad_gain_two,
    )


def solution(mesh):
    both = ("dp", "fsdp")
    sequences = P(None, both, None, None)
    rows = P(both, None)
    in_specs = (sequences, P(), P()) + (rows,) * 7 + (P(both), P(both), sequences)
    out_specs = (sequences, sequences) + (rows,) * 7 + (P(both), P(both))
    return jax.shard_map(
        per_device, mesh=mesh, in_specs=in_specs, out_specs=out_specs, check_vma=False
    )
```

```python
import math

import jax
import jax.numpy as jnp
from jax import lax
from jax.experimental import pallas as pl
from jax.experimental.pallas import tpu as pltpu
from jax.sharding import PartitionSpec as P

H = 16
HD = 128
EPSILON = 1e-05
F32 = jnp.float32
BF16 = jnp.bfloat16
BOTH = ("dp", "fsdp")
CORE, X, Y = 1, 2, 4
ROWS = 512
SHRINK = 50
VMEM_BYTES = 60 * 1024 * 1024


def rope_tables(length_cap, repeats):
    halfway = HD // 2
    position = jnp.arange(length_cap, dtype=F32)
    inverse = 10000.0 ** (-2.0 * jnp.arange(halfway, dtype=F32) / HD)
    angles = position[:, None] * inverse[None, :]
    cosine, sine = jnp.cos(angles), jnp.sin(angles)
    cosine = jnp.concatenate([cosine, cosine], axis=1)
    sine = jnp.concatenate([-sine, sine], axis=1)
    return jnp.tile(cosine, (repeats, 1)), jnp.tile(sine, (repeats, 1))


def dot_nn(left, right):
    return lax.dot_general(left, right, (((1,), (0,)), ((), ())), preferred_element_type=F32)


def dot_nt(left, right):
    return lax.dot_general(left, right, (((1,), (1,)), ((), ())), preferred_element_type=F32)


def dot_tn(left, right):
    return lax.dot_general(left, right, (((0,), (0,)), ((), ())), preferred_element_type=F32)


def whole_spec(array):
    return pl.BlockSpec(array.shape, lambda i, *_: (0,) * array.ndim, pipeline_mode=pl.Buffered(1))


def part_specs(count, steps, columns):
    def spec(k):
        return pl.BlockSpec(
            (ROWS, columns), lambda i, *_: (jnp.clip(i - k * steps, 0, steps - 1), 0)
        )

    return [spec(k) for k in range(count)]


def row_spec(columns):
    return pl.BlockSpec((ROWS, columns), lambda i, *_: (i, 0))


def by_part(count, steps, work):
    if count == 1:
        work(0)
        return
    for k in range(count):
        pl.when(pl.program_id(0) // steps == k)(lambda k=k: work(k))


def tiles(extent, size):
    size = min(size, extent)
    return [slice(at, at + size) for at in range(0, extent, size)]


def call(body, name, parts, rows, whole, scalars, part_outs, row_outs, flops, scratch=(), shrink=SHRINK):
    count = len(parts)
    steps = parts[0].shape[0] // ROWS if parts else rows[0].shape[0] // ROWS
    cuts = count if parts else 1
    total = steps * max(cuts, 1)
    out_shape, out_specs = [], []
    for columns, dtype, pieces in part_outs:
        per = total // pieces
        out_shape += [jax.ShapeDtypeStruct((per * ROWS, columns), dtype)] * pieces
        out_specs += part_specs(pieces, per, columns)
    for columns, dtype in row_outs:
        out_shape.append(jax.ShapeDtypeStruct((total * ROWS, columns), dtype))
        out_specs.append(row_spec(columns))
    in_specs = part_specs(count, steps, parts[0].shape[1]) if parts else []
    in_specs += [row_spec(r.shape[1]) for r in rows] + [whole_spec(w) for w in whole]
    moved = sum(a.size * a.dtype.itemsize for a in list(parts) + list(rows) + list(whole))
    moved += sum(math.prod(o.shape) * jnp.dtype(o.dtype).itemsize for o in out_shape)
    return pl.pallas_call(
        body,
        out_shape=out_shape,
        grid_spec=pltpu.PrefetchScalarGridSpec(
            num_scalar_prefetch=len(scalars), grid=(total,), in_specs=in_specs, out_specs=out_specs,
            scratch_shapes=list(scratch),
        ),
        compiler_params=pltpu.CompilerParams(
            dimension_semantics=("arbitrary",), vmem_limit_bytes=VMEM_BYTES
        ),
        cost_estimate=pl.CostEstimate(flops=flops // shrink, bytes_accessed=moved // shrink, transcendentals=0),
        name=name,
    )(*scalars, *parts, *rows, *whole)


def turn(value, cosine, sine):
    return value * cosine + pltpu.roll(value, HD // 2, 1) * sine


def allowed_of(live, cap):
    row = lax.broadcasted_iota(jnp.int32, (cap, cap), 0)
    column = lax.broadcasted_iota(jnp.int32, (cap, cap), 1)
    return (row >= column) & (column < live)


def attention_forward(parts, live, wqkv, wo, cosine, sine, cap):
    count, cols, width = len(parts), wo.shape[0], wo.shape[1]
    steps = parts[0].shape[0] // ROWS
    scale, shift = 1.0 / math.sqrt(HD), -math.log(cap)

    def body(live_ref, *refs):
        sources, refs = refs[:count], refs[count:]
        wqkv_ref, wo_ref, cos_ref, sin_ref = refs[:4]
        outs, (qkv_ref, mixed_ref) = refs[4 : 4 + count], refs[4 + count :]
        step = pl.program_id(0)

        def project(part):
            rows = sources[part][...]
            for kind in range(3):
                value = dot_nn(rows, wqkv_ref[:, kind * cols : (kind + 1) * cols])
                for head in tiles(cols, HD):
                    one = value[:, head]
                    if kind < 2:
                        one = turn(one, cos_ref[...], sin_ref[...])
                    at = slice(kind * cols + head.start, kind * cols + head.stop)
                    qkv_ref[:, at] = one.astype(BF16)

        by_part(count, steps, project)
        for k, sequence in enumerate(tiles(ROWS, cap)):
            allowed = allowed_of(live_ref[step * (ROWS // cap) + k], cap)
            for head in tiles(cols, HD):
                query = qkv_ref[sequence, head]
                key = qkv_ref[sequence, cols + head.start : cols + head.stop]
                value = qkv_ref[sequence, 2 * cols + head.start : 2 * cols + head.stop]
                gates = jax.nn.sigmoid(dot_nt(query, key) * scale + shift)
                probs = jnp.where(allowed, gates, 0.0).astype(BF16)
                mixed_ref[sequence, head] = dot_nn(probs, value).astype(BF16)

        def finish(part):
            outs[part][...] = dot_nn(mixed_ref[...], wo_ref[...]).astype(BF16)

        by_part(count, steps, finish)

    total = count * steps * ROWS
    out = call(
        body,
        "attention_forward",
        parts,
        [],
        [wqkv, wo, cosine, sine],
        [live],
        [(width, BF16, count)],
        [(3 * cols, BF16), (cols, BF16)],
        2 * total * width * 4 * cols,
    )
    return out[:count], out[count], out[count + 1]


def attention_backward(parts, live, qkv, wqkv, wo, cosine, sine, cap):
    count, cols, width = len(parts), wo.shape[0], wo.shape[1]
    steps = parts[0].shape[0] // ROWS
    scale, shift = 1.0 / math.sqrt(HD), -math.log(cap)

    def body(live_ref, *refs):
        sources, refs = refs[:count], refs[count:]
        qkv_ref, wqkv_ref, wo_ref, cos_ref, sin_ref = refs[:5]
        outs, (back_ref, mixed_ref) = refs[5 : 5 + count], refs[5 + count :]
        step = pl.program_id(0)

        def enter(part):
            mixed_ref[...] = dot_nt(sources[part][...], wo_ref[...]).astype(BF16)

        by_part(count, steps, enter)
        for k, sequence in enumerate(tiles(ROWS, cap)):
            allowed = allowed_of(live_ref[step * (ROWS // cap) + k], cap)
            cosine_here, sine_here = cos_ref[sequence, :], sin_ref[sequence, :]
            for head in tiles(cols, HD):
                key_at = slice(cols + head.start, cols + head.stop)
                value_at = slice(2 * cols + head.start, 2 * cols + head.stop)
                query, key, value = (
                    qkv_ref[sequence, at] for at in (head, key_at, value_at)
                )
                grad = mixed_ref[sequence, head]
                gates = jax.nn.sigmoid(dot_nt(query, key) * scale + shift)
                probs = jnp.where(allowed, gates, 0.0).astype(BF16)
                grad_logits = dot_nt(grad, value) * gates * (1.0 - gates)
                grad_logits = jnp.where(allowed, grad_logits, 0.0).astype(BF16)
                grad_query = dot_nn(grad_logits, key) * scale
                grad_key = dot_tn(grad_logits, query) * scale
                back_ref[sequence, head] = turn(grad_query, cosine_here, -sine_here).astype(BF16)
                back_ref[sequence, key_at] = turn(grad_key, cosine_here, -sine_here).astype(BF16)
                back_ref[sequence, value_at] = dot_tn(probs, grad).astype(BF16)

        def finish(part):
            outs[part][...] = dot_nt(back_ref[...], wqkv_ref[...]).astype(BF16)

        by_part(count, steps, finish)

    total = count * steps * ROWS
    out = call(
        body,
        "attention_backward",
        parts,
        [qkv],
        [wqkv, wo, cosine, sine],
        [live],
        [(width, BF16, count)],
        [(3 * cols, BF16)],
        2 * total * width * 4 * cols,
        [pltpu.VMEM((ROWS, cols), BF16)],
        1,
    )
    return out[:count], out[count]


def feed_forward(parts, wgu):
    count, width = len(parts), wgu.shape[0]
    share = wgu.shape[1] // 2
    steps = parts[0].shape[0] // ROWS

    def body(*refs):
        sources, (wgu_ref, gate_ref, up_ref, active_ref) = refs[:count], refs[count:]

        def work(part):
            rows = sources[part][...]
            for at in tiles(share, 256):
                gate = dot_nn(rows, wgu_ref[:, at])
                up = dot_nn(rows, wgu_ref[:, share + at.start : share + at.stop])
                gate_ref[:, at] = gate
                up_ref[:, at] = up
                active_ref[:, at] = (gate * jax.nn.sigmoid(gate) * up).astype(BF16)

        by_part(count, steps, work)

    total = count * steps * ROWS
    return call(
        body,
        "feed_forward",
        parts,
        [],
        [wgu],
        [],
        [],
        [(share, F32), (share, F32), (share, BF16)],
        4 * total * width * share,
    )


def feed_back(parts, gate, up, wd, wgu):
    count, width = len(parts), wgu.shape[0]
    share = wgu.shape[1] // 2
    steps = parts[0].shape[0] // ROWS

    def body(*refs):
        sources, refs = refs[:count], refs[count:]
        gate_ref, up_ref, wd_ref, wgu_ref = refs[:4]
        outs, (grad_ref,) = refs[4 : 4 + count], refs[4 + count :]

        def work(part):
            rows = sources[part][...]
            for at in tiles(share, 256):
                grad = dot_nn(rows, wd_ref[:, at])
                gate = gate_ref[:, at]
                open_gate = jax.nn.sigmoid(gate)
                grad_gate = grad * up_ref[:, at] * (open_gate * (1.0 + gate * (1.0 - open_gate)))
                grad_ref[:, at] = grad_gate.astype(BF16)
                grad_up = grad * (gate * open_gate)
                grad_ref[:, share + at.start : share + at.stop] = grad_up.astype(BF16)
            grads = grad_ref[...]
            for at in tiles(width, 512):
                outs[part][:, at] = dot_nt(grads, wgu_ref[at, :]).astype(BF16)

        by_part(count, steps, work)

    total = count * steps * ROWS
    out = call(
        body,
        "feed_back",
        parts,
        [gate, up],
        [wd, wgu],
        [],
        [(width, BF16, count)],
        [(2 * share, BF16)],
        6 * total * width * share,
    )
    return out[:count], out[count]


def feed_down(active, wd, pieces):
    width = wd.shape[0]
    steps = active.shape[0] // ROWS // pieces

    def body(active_ref, wd_ref, *outs):
        def work(part):
            rows = active_ref[...]
            for at in tiles(width, 512):
                outs[part][:, at] = dot_nt(rows, wd_ref[at, :]).astype(BF16)

        by_part(pieces, steps, work)

    return call(
        body,
        "feed_down",
        [],
        [active],
        [wd],
        [],
        [(width, BF16, pieces)],
        [],
        2 * active.size * width,
        shrink=1,
    )


def outer(lefts, rights, block, shrink=SHRINK):
    parts = max(len(lefts), len(rights))
    rows = lefts[0].shape[0] * len(lefts) // parts
    height, width = lefts[0].shape[1], rights[0].shape[1]
    nleft = len(lefts)

    def body(*refs):
        def pieces(group):
            if len(group) == parts:
                return [ref[...] for ref in group]
            return [group[0][k * rows : (k + 1) * rows, :] for k in range(parts)]

        left, right = pieces(refs[:nleft]), pieces(refs[nleft:-1])
        total = dot_tn(left[0], right[0])
        for one, other in zip(left[1:], right[1:], strict=True):
            total += dot_tn(one, other)
        refs[-1][...] = total.astype(BF16)

    return pl.pallas_call(
        body,
        out_shape=jax.ShapeDtypeStruct((height, width), BF16),
        grid=(height // block,),
        in_specs=[pl.BlockSpec((a.shape[0], block), lambda i: (0, i)) for a in lefts]
        + [whole_spec(b) for b in rights],
        out_specs=pl.BlockSpec((block, width), lambda i: (i, 0)),
        compiler_params=pltpu.CompilerParams(
            dimension_semantics=("arbitrary",), vmem_limit_bytes=VMEM_BYTES
        ),
        cost_estimate=pl.CostEstimate(
            flops=2 * parts * rows * height * width // shrink,
            bytes_accessed=2 * (parts * rows * (height + width) + height * width) // shrink,
            transcendentals=0,
        ),
        name="outer",
    )(*lefts, *rights)


def finish(pieces, weights, gain, moves):
    count, rows = len(weights), gain.shape[0]

    def body(*refs):
        pieces_ref, gain_ref, weight_refs = refs[0], refs[1], refs[2 : 2 + count]
        outs, total_ref = refs[2 + count : -1], refs[-1]
        scale = gain_ref[...]
        total = jnp.zeros((rows, HD), F32)
        for sender, source, which, target in moves:
            value = pieces_ref[sender, :, source].astype(F32)
            outs[which][:, target] = value * scale
            product = value * weight_refs[which][:, target].astype(F32)
            for at in tiles(product.shape[1], HD):
                total += product[:, at]
        total_ref[...] = jnp.broadcast_to(jnp.sum(total, axis=1, keepdims=True), (rows, HD))

    out = pl.pallas_call(
        body,
        out_shape=[jax.ShapeDtypeStruct(w.shape, F32) for w in weights]
        + [jax.ShapeDtypeStruct((rows, HD), F32)],
        cost_estimate=pl.CostEstimate(
            flops=pieces.size // SHRINK, bytes_accessed=pieces.size // SHRINK, transcendentals=0
        ),
        compiler_params=pltpu.CompilerParams(vmem_limit_bytes=VMEM_BYTES),
        name="finish",
    )(pieces, gain, *weights)
    return out[:-1], out[-1][:, 0]


def after(value, *earlier):
    return lax.optimization_barrier((value,) + earlier)[0]


def swap(value, mask):
    count = lax.axis_size("dp") * lax.axis_size("fsdp")
    return lax.ppermute(value, BOTH, [(i, i ^ mask) for i in range(count)])


def add_low(left, right):
    return (left.astype(F32) + right.astype(F32)).astype(BF16)


def is_paired():
    return lax.axis_size("dp") == 4 and lax.axis_size("fsdp") == 8


def order_of(first, second):
    return ((0, first, second, first | second), (0, second, first, first | second))


def gather_group(rows, first, second, *meanwhile):
    if not is_paired():
        whole = lax.all_gather(rows, "fsdp", axis=1)
        return [whole.reshape(-1, rows.shape[-1])]
    a, b = rows[0], rows[1]
    a1, b2 = swap(a, first), swap(b, second)
    a2, b1 = swap(a, second), swap(b, first)
    a3, b3 = swap(a1, second), swap(b2, first)
    own = jnp.concatenate([a, a1, a2, a3, b, b2, b1, b3], axis=0)
    return [own, swap(after(own, *meanwhile) if meanwhile else own, CORE)]


def scatter_group(parts, first, second, like, fill=None):
    if not is_paired():
        micro, length, width = like.shape
        blocks = parts[0].reshape(micro, -1, length, width)
        if fill is not None:
            fill(lambda value: value)
        return lax.psum_scatter(blocks, "fsdp", scatter_dimension=1).astype(F32)
    keep, send = (part.reshape((2, 4) + like.shape[1:]) for part in parts)
    got = swap(send, CORE)
    a, a_far = add_low(keep[0, :2], got[0, :2]), add_low(keep[0, 2:], got[0, 2:])
    b, b_far = add_low(keep[1, :2], got[1, :2]), add_low(keep[1, 2:], got[1, 2:])
    if fill is not None:
        fill(lambda value: after(value, a_far, b_far))
    a_got, b_got = swap(a_far, second), swap(b_far, first)
    a, a_far = add_low(a[0], a_got[0]), add_low(a[1], a_got[1])
    b, b_far = add_low(b[0], b_got[0]), add_low(b[1], b_got[1])
    a_got, b_got = swap(a_far, first), swap(b_far, second)
    return jnp.stack([a.astype(F32) + a_got.astype(F32), b.astype(F32) + b_got.astype(F32)])


def per_device(
    tokens,
    lengths,
    order,
    w_query,
    w_key,
    w_value,
    w_output,
    w_gate,
    w_up,
    w_down,
    gain_attn,
    gain_ffn,
    cotangent,
):
    groups, members = lax.axis_size("dp"), lax.axis_size("fsdp")
    plane, member = lax.axis_index("dp"), lax.axis_index("fsdp")
    paired = is_paired()
    micro, _, cap, width = tokens.shape
    own_rows = w_query.shape[0]
    hidden = w_gate.shape[1]
    share = hidden // members
    sharers = HD // own_rows
    kinds = members // sharers
    my_heads = groups // sharers
    head_cols = my_heads * HD

    slots = jnp.arange(order.shape[1], dtype=jnp.int32)
    me = plane * members + member
    position = jnp.arange(cap, dtype=jnp.int32)

    if paired:
        block = jnp.array(
            [mask | core for core in (0, CORE) for masks in order_of(X, Y) for mask in masks]
        )
        devices = (me ^ block).reshape(2, 2, 4)
    else:
        devices = jnp.broadcast_to(plane * members + jnp.arange(members), (1, micro, members))
    placed = jnp.sum(
        jnp.where(devices[..., None] == slots, order[None, :, None, :], 0), axis=-1
    )
    lives = jnp.sum(
        jnp.where(placed[..., None] == slots, lengths[None, :, None, :], 0), axis=-1
    ).reshape(-1)

    my_slot = jnp.sum(jnp.where(slots == me, order, 0), axis=-1)
    my_live = jnp.sum(jnp.where(slots == my_slot[:, None], lengths, 0), axis=-1)
    my_mask = (position < my_live[:, None]).astype(F32)[:, :, None]

    gain_one = gain_attn.astype(F32)[:, None]
    gain_two = gain_ffn.astype(F32)[:, None]

    def scaled(weight, gain):
        return (weight.astype(F32) * gain).astype(BF16)

    def by_head(weight):
        cut = weight.reshape(own_rows, sharers, my_heads, kinds, HD)
        return cut.transpose(3, 1, 0, 2, 4).reshape(members, own_rows, head_cols)

    def by_unit(weight):
        return weight.reshape(own_rows, members, share).transpose(1, 0, 2)

    def planes(value):
        return lax.all_gather(value, "dp", axis=0, tiled=True)

    def over_planes(value):
        return lax.psum_scatter(value, "dp", scatter_dimension=0, tiled=True)

    def spread(pieces):
        count, rows, columns = pieces.shape
        flat = pieces.reshape(count * rows, columns)
        return lax.all_to_all(flat, "fsdp", 0, 0, tiled=True)

    cut_qkv = jnp.concatenate(
        [by_head(scaled(w, gain_one)) for w in (w_query, w_key, w_value)], axis=2
    )
    cut_gu = jnp.concatenate([by_unit(scaled(w, gain_two)) for w in (w_gate, w_up)], axis=2)
    cut_d = by_unit(w_down)
    near_qkv = spread(cut_qkv)
    wqkv = planes(near_qkv)
    raw = planes(w_output).reshape(sharers, my_heads, own_rows, width)
    subgroups = [[s * sharers + i for i in range(sharers)] for s in range(kinds)]

    def exchange(value):
        if not paired:
            return lax.all_to_all(value, "fsdp", 0, 0, axis_index_groups=subgroups)
        odd = (member & CORE) != 0
        mine, send = jnp.where(odd, value[1], value[0]), jnp.where(odd, value[0], value[1])
        got = swap(send, CORE)
        return jnp.stack([jnp.where(odd, got, mine), jnp.where(odd, mine, got)])

    wo = exchange(raw).transpose(1, 0, 2, 3).reshape(head_cols, width)

    x = after(tokens, near_qkv)[:, 0].astype(F32)
    inverse_one = lax.rsqrt(jnp.mean(x * x, axis=-1, keepdims=True) + EPSILON)
    normal_one = x * inverse_one
    n1 = gather_group(normal_one.astype(BF16), X, Y)
    near_gu = spread(after(cut_gu, near_qkv))
    upstream = cotangent[:, 0].astype(F32) * my_mask
    returned_grad = gather_group(after(upstream.astype(BF16), n1[0], near_gu), X, Y)
    near_d = spread(after(cut_d, returned_grad[0]))
    wgu, wd = planes(near_gu), planes(near_d)
    n1[0] = after(n1[0], near_gu)

    cosine, sine = rope_tables(cap, ROWS // cap)
    parts, qkv, mixed = attention_forward(n1, lives, wqkv, wo, cosine, sine, cap)
    parts = [*parts[:-1], after(parts[-1], *returned_grad)]
    attended = scatter_group(parts, X, Y, x)
    hidden_one = x + attended

    inverse_two = lax.rsqrt(jnp.mean(hidden_one * hidden_one, axis=-1, keepdims=True) + EPSILON)
    normal_two = hidden_one * inverse_two
    n2 = gather_group(normal_two.astype(BF16), X, Y, wgu)
    gate, up, activated = feed_forward(n2, wgu)

    part_d = outer(returned_grad, [activated], ROWS)
    returned_grad = list(lax.optimization_barrier((*returned_grad, part_d))[:-1])
    sum_d = over_planes(part_d)
    parts, grad_gu = feed_back(returned_grad, gate, up, wd, wgu)
    travelling = {}

    def fill(tie):
        travelling["gu"] = outer([tie(n2[0]), *n2[1:]], [grad_gu], ROWS, 1)

    back_two = after(scatter_group(parts, X, Y, x, fill), travelling["gu"], sum_d)
    sum_gu = over_planes(travelling["gu"])
    grad_hidden = upstream + inverse_two * (
        back_two - normal_two * jnp.mean(back_two * normal_two, axis=-1, keepdims=True)
    )
    grad_low = grad_hidden.astype(BF16)
    def home(mine):
        return lax.all_to_all(mine, "fsdp", 0, 0, tiled=True).reshape(members, own_rows, -1)

    grad_attended = gather_group(grad_low, X, Y)
    part_o = outer([mixed], grad_attended, HD)
    ties = []
    parts = feed_down(after(activated, grad_low), wd, len(n2))
    returned = scatter_group(parts, X, Y, x, ties.append)
    grad_attended = [ties[0](after(grad_attended[0], part_o)), *grad_attended[1:]]
    parts, grad_qkv = attention_backward(grad_attended, lives, qkv, wqkv, wo, cosine, sine, cap)
    part_o = exchange(part_o.reshape(my_heads, sharers, own_rows, width).transpose(1, 0, 2, 3))
    part_qkv = outer(n1, [grad_qkv], ROWS, 1)
    grad_wo = over_planes(after(part_o.reshape(groups * own_rows, width), sum_gu, part_qkv))
    sum_qkv = over_planes(after(part_qkv, sum_gu))
    sum_d, returned = lax.optimization_barrier((sum_d, returned))
    output = ((hidden_one + returned) * my_mask).astype(BF16)
    sum_dgu = home(jnp.concatenate([sum_d, after(sum_gu, part_qkv)], axis=1))
    back_one = scatter_group(parts, X, Y, x)
    back_one, sum_dgu = lax.optimization_barrier((back_one, sum_dgu))
    sum_d, sum_gu = sum_dgu[:, :, :share], sum_dgu[:, :, share:]
    grad_tokens = (
        grad_hidden
        + inverse_one
        * (back_one - normal_one * jnp.mean(back_one * normal_one, axis=-1, keepdims=True))
    ).astype(BF16)

    sum_qkv = home(after(sum_qkv, sum_dgu))

    def from_units(value):
        return value.transpose(1, 0, 2).reshape(own_rows, hidden).astype(F32)

    moves_qkv = [
        (
            p * sharers + c,
            slice(kind * head_cols + m * HD, kind * head_cols + (m + 1) * HD),
            kind,
            slice(((c * my_heads + m) * kinds + p) * HD, ((c * my_heads + m) * kinds + p + 1) * HD),
        )
        for kind in range(3)
        for p in range(kinds)
        for c in range(sharers)
        for m in range(my_heads)
    ]
    grad_qkv, grad_gain_one = finish(sum_qkv, (w_query, w_key, w_value), gain_one, moves_qkv)
    raw_gu = [from_units(sum_gu[:, :, i * share : (i + 1) * share]) for i in range(2)]
    grad_gain_two = sum(
        jnp.sum(g * w.astype(F32), axis=1) for g, w in zip(raw_gu, (w_gate, w_up), strict=True)
    )
    return (
        output[:, None],
        grad_tokens[:, None],
        *grad_qkv,
        grad_wo.astype(F32),
        raw_gu[0] * gain_two,
        raw_gu[1] * gain_two,
        from_units(sum_d),
        grad_gain_one,
        grad_gain_two,
    )


def solution(mesh):
    sequences = P(None, BOTH, None, None)
    rows = P(BOTH, None)
    in_specs = (sequences, P(), P()) + (rows,) * 7 + (P(BOTH), P(BOTH), sequences)
    out_specs = (sequences, sequences) + (rows,) * 7 + (P(BOTH), P(BOTH))
    return jax.shard_map(
        per_device, mesh=mesh, in_specs=in_specs, out_specs=out_specs, check_vma=False
    )
```

```python
import math

import jax
import jax.numpy as jnp
from jax import lax
from jax.experimental import pallas as pl
from jax.experimental.pallas import tpu as pltpu
from jax.sharding import PartitionSpec as P

H = 16
HD = 128
EPSILON = 1e-05
F32 = jnp.float32
BF16 = jnp.bfloat16
BOTH = ("dp", "fsdp")
CORE, X, Y = 1, 2, 4
ROWS = 512
SHRINK = 50
VMEM_BYTES = 60 * 1024 * 1024


def rope_tables(length_cap, repeats):
    halfway = HD // 2
    position = jnp.arange(length_cap, dtype=F32)
    inverse = 10000.0 ** (-2.0 * jnp.arange(halfway, dtype=F32) / HD)
    angles = position[:, None] * inverse[None, :]
    cosine, sine = jnp.cos(angles), jnp.sin(angles)
    cosine = jnp.concatenate([cosine, cosine], axis=1)
    sine = jnp.concatenate([-sine, sine], axis=1)
    return jnp.tile(cosine, (repeats, 1)), jnp.tile(sine, (repeats, 1))


def dot_nn(left, right):
    return lax.dot_general(left, right, (((1,), (0,)), ((), ())), preferred_element_type=F32)


def dot_nt(left, right):
    return lax.dot_general(left, right, (((1,), (1,)), ((), ())), preferred_element_type=F32)


def dot_tn(left, right):
    return lax.dot_general(left, right, (((0,), (0,)), ((), ())), preferred_element_type=F32)


def whole_spec(array):
    return pl.BlockSpec(array.shape, lambda i, *_: (0,) * array.ndim, pipeline_mode=pl.Buffered(1))


def part_specs(count, steps, columns):
    def spec(k):
        return pl.BlockSpec(
            (ROWS, columns), lambda i, *_: (jnp.clip(i - k * steps, 0, steps - 1), 0)
        )

    return [spec(k) for k in range(count)]


def row_spec(columns):
    return pl.BlockSpec((ROWS, columns), lambda i, *_: (i, 0))


def by_part(count, steps, work):
    if count == 1:
        work(0)
        return
    for k in range(count):
        pl.when(pl.program_id(0) // steps == k)(lambda k=k: work(k))


def tiles(extent, size):
    size = min(size, extent)
    return [slice(at, at + size) for at in range(0, extent, size)]


def call(body, name, parts, rows, whole, scalars, part_outs, row_outs, flops, scratch=(), shrink=SHRINK):
    count = len(parts)
    steps = parts[0].shape[0] // ROWS if parts else rows[0].shape[0] // ROWS
    cuts = count if parts else 1
    total = steps * max(cuts, 1)
    out_shape, out_specs = [], []
    for columns, dtype, pieces in part_outs:
        per = total // pieces
        out_shape += [jax.ShapeDtypeStruct((per * ROWS, columns), dtype)] * pieces
        out_specs += part_specs(pieces, per, columns)
    for columns, dtype in row_outs:
        out_shape.append(jax.ShapeDtypeStruct((total * ROWS, columns), dtype))
        out_specs.append(row_spec(columns))
    in_specs = part_specs(count, steps, parts[0].shape[1]) if parts else []
    in_specs += [row_spec(r.shape[1]) for r in rows] + [whole_spec(w) for w in whole]
    moved = sum(a.size * a.dtype.itemsize for a in list(parts) + list(rows) + list(whole))
    moved += sum(math.prod(o.shape) * jnp.dtype(o.dtype).itemsize for o in out_shape)
    return pl.pallas_call(
        body,
        out_shape=out_shape,
        grid_spec=pltpu.PrefetchScalarGridSpec(
            num_scalar_prefetch=len(scalars), grid=(total,), in_specs=in_specs, out_specs=out_specs,
            scratch_shapes=list(scratch),
        ),
        compiler_params=pltpu.CompilerParams(
            dimension_semantics=("arbitrary",), vmem_limit_bytes=VMEM_BYTES
        ),
        cost_estimate=pl.CostEstimate(flops=flops // shrink, bytes_accessed=moved // shrink, transcendentals=0),
        name=name,
    )(*scalars, *parts, *rows, *whole)


def turn(value, cosine, sine):
    return value * cosine + pltpu.roll(value, HD // 2, 1) * sine


def allowed_of(live, cap):
    row = lax.broadcasted_iota(jnp.int32, (cap, cap), 0)
    column = lax.broadcasted_iota(jnp.int32, (cap, cap), 1)
    return (row >= column) & (column < live)


def attention_forward(parts, live, wqkv, wo, cosine, sine, cap):
    count, cols, width = len(parts), wo.shape[0], wo.shape[1]
    steps = parts[0].shape[0] // ROWS
    scale, shift = 1.0 / math.sqrt(HD), -math.log(cap)

    def body(live_ref, *refs):
        sources, refs = refs[:count], refs[count:]
        wqkv_ref, wo_ref, cos_ref, sin_ref = refs[:4]
        outs, (qkv_ref, mixed_ref) = refs[4 : 4 + count], refs[4 + count :]
        step = pl.program_id(0)

        def project(part):
            rows = sources[part][...]
            for kind in range(3):
                value = dot_nn(rows, wqkv_ref[:, kind * cols : (kind + 1) * cols])
                for head in tiles(cols, HD):
                    one = value[:, head]
                    if kind < 2:
                        one = turn(one, cos_ref[...], sin_ref[...])
                    at = slice(kind * cols + head.start, kind * cols + head.stop)
                    qkv_ref[:, at] = one.astype(BF16)

        by_part(count, steps, project)
        for k, sequence in enumerate(tiles(ROWS, cap)):
            allowed = allowed_of(live_ref[step * (ROWS // cap) + k], cap)
            for head in tiles(cols, HD):
                query = qkv_ref[sequence, head]
                key = qkv_ref[sequence, cols + head.start : cols + head.stop]
                value = qkv_ref[sequence, 2 * cols + head.start : 2 * cols + head.stop]
                gates = jax.nn.sigmoid(dot_nt(query, key) * scale + shift)
                probs = jnp.where(allowed, gates, 0.0).astype(BF16)
                mixed_ref[sequence, head] = dot_nn(probs, value).astype(BF16)

        def finish(part):
            outs[part][...] = dot_nn(mixed_ref[...], wo_ref[...]).astype(BF16)

        by_part(count, steps, finish)

    total = count * steps * ROWS
    out = call(
        body,
        "attention_forward",
        parts,
        [],
        [wqkv, wo, cosine, sine],
        [live],
        [(width, BF16, count)],
        [(3 * cols, BF16), (cols, BF16)],
        2 * total * width * 4 * cols,
    )
    return out[:count], out[count], out[count + 1]


def attention_backward(parts, live, qkv, wqkv, wo, cosine, sine, cap):
    count, cols, width = len(parts), wo.shape[0], wo.shape[1]
    steps = parts[0].shape[0] // ROWS
    scale, shift = 1.0 / math.sqrt(HD), -math.log(cap)

    def body(live_ref, *refs):
        sources, refs = refs[:count], refs[count:]
        qkv_ref, wqkv_ref, wo_ref, cos_ref, sin_ref = refs[:5]
        outs, (back_ref, mixed_ref) = refs[5 : 5 + count], refs[5 + count :]
        step = pl.program_id(0)

        def enter(part):
            mixed_ref[...] = dot_nt(sources[part][...], wo_ref[...]).astype(BF16)

        by_part(count, steps, enter)
        for k, sequence in enumerate(tiles(ROWS, cap)):
            allowed = allowed_of(live_ref[step * (ROWS // cap) + k], cap)
            cosine_here, sine_here = cos_ref[sequence, :], sin_ref[sequence, :]
            for head in tiles(cols, HD):
                key_at = slice(cols + head.start, cols + head.stop)
                value_at = slice(2 * cols + head.start, 2 * cols + head.stop)
                query, key, value = (
                    qkv_ref[sequence, at] for at in (head, key_at, value_at)
                )
                grad = mixed_ref[sequence, head]
                gates = jax.nn.sigmoid(dot_nt(query, key) * scale + shift)
                probs = jnp.where(allowed, gates, 0.0).astype(BF16)
                grad_logits = dot_nt(grad, value) * gates * (1.0 - gates)
                grad_logits = jnp.where(allowed, grad_logits, 0.0).astype(BF16)
                grad_query = dot_nn(grad_logits, key) * scale
                grad_key = dot_tn(grad_logits, query) * scale
                back_ref[sequence, head] = turn(grad_query, cosine_here, -sine_here).astype(BF16)
                back_ref[sequence, key_at] = turn(grad_key, cosine_here, -sine_here).astype(BF16)
                back_ref[sequence, value_at] = dot_tn(probs, grad).astype(BF16)

        def finish(part):
            outs[part][...] = dot_nt(back_ref[...], wqkv_ref[...]).astype(BF16)

        by_part(count, steps, finish)

    total = count * steps * ROWS
    out = call(
        body,
        "attention_backward",
        parts,
        [qkv],
        [wqkv, wo, cosine, sine],
        [live],
        [(width, BF16, count)],
        [(3 * cols, BF16)],
        2 * total * width * 4 * cols,
        [pltpu.VMEM((ROWS, cols), BF16)],
        1,
    )
    return out[:count], out[count]


def feed_forward(parts, wgu):
    count, width = len(parts), wgu.shape[0]
    share = wgu.shape[1] // 2
    steps = parts[0].shape[0] // ROWS

    def body(*refs):
        sources, (wgu_ref, gate_ref, up_ref, active_ref) = refs[:count], refs[count:]

        def work(part):
            rows = sources[part][...]
            for at in tiles(share, 256):
                gate = dot_nn(rows, wgu_ref[:, at])
                up = dot_nn(rows, wgu_ref[:, share + at.start : share + at.stop])
                gate_ref[:, at] = gate
                up_ref[:, at] = up
                active_ref[:, at] = (gate * jax.nn.sigmoid(gate) * up).astype(BF16)

        by_part(count, steps, work)

    total = count * steps * ROWS
    return call(
        body,
        "feed_forward",
        parts,
        [],
        [wgu],
        [],
        [],
        [(share, F32), (share, F32), (share, BF16)],
        4 * total * width * share,
    )


def feed_back(parts, gate, up, wd, wgu):
    count, width = len(parts), wgu.shape[0]
    share = wgu.shape[1] // 2
    steps = parts[0].shape[0] // ROWS

    def body(*refs):
        sources, refs = refs[:count], refs[count:]
        gate_ref, up_ref, wd_ref, wgu_ref = refs[:4]
        outs, (grad_ref,) = refs[4 : 4 + count], refs[4 + count :]

        def work(part):
            rows = sources[part][...]
            for at in tiles(share, 256):
                grad = dot_nn(rows, wd_ref[:, at])
                gate = gate_ref[:, at]
                open_gate = jax.nn.sigmoid(gate)
                grad_gate = grad * up_ref[:, at] * (open_gate * (1.0 + gate * (1.0 - open_gate)))
                grad_ref[:, at] = grad_gate.astype(BF16)
                grad_up = grad * (gate * open_gate)
                grad_ref[:, share + at.start : share + at.stop] = grad_up.astype(BF16)
            grads = grad_ref[...]
            for at in tiles(width, 512):
                outs[part][:, at] = dot_nt(grads, wgu_ref[at, :]).astype(BF16)

        by_part(count, steps, work)

    total = count * steps * ROWS
    out = call(
        body,
        "feed_back",
        parts,
        [gate, up],
        [wd, wgu],
        [],
        [(width, BF16, count)],
        [(2 * share, BF16)],
        6 * total * width * share,
    )
    return out[:count], out[count]


def feed_down(active, wd, pieces):
    width = wd.shape[0]
    steps = active.shape[0] // ROWS // pieces

    def body(active_ref, wd_ref, *outs):
        def work(part):
            rows = active_ref[...]
            for at in tiles(width, 512):
                outs[part][:, at] = dot_nt(rows, wd_ref[at, :]).astype(BF16)

        by_part(pieces, steps, work)

    return call(
        body,
        "feed_down",
        [],
        [active],
        [wd],
        [],
        [(width, BF16, pieces)],
        [],
        2 * active.size * width,
        shrink=1,
    )


def outer(lefts, rights, block, shrink=SHRINK):
    parts = max(len(lefts), len(rights))
    rows = lefts[0].shape[0] * len(lefts) // parts
    height, width = lefts[0].shape[1], rights[0].shape[1]
    nleft = len(lefts)

    def body(*refs):
        def pieces(group):
            if len(group) == parts:
                return [ref[...] for ref in group]
            return [group[0][k * rows : (k + 1) * rows, :] for k in range(parts)]

        left, right = pieces(refs[:nleft]), pieces(refs[nleft:-1])
        total = dot_tn(left[0], right[0])
        for one, other in zip(left[1:], right[1:], strict=True):
            total += dot_tn(one, other)
        refs[-1][...] = total.astype(BF16)

    return pl.pallas_call(
        body,
        out_shape=jax.ShapeDtypeStruct((height, width), BF16),
        grid=(height // block,),
        in_specs=[pl.BlockSpec((a.shape[0], block), lambda i: (0, i)) for a in lefts]
        + [whole_spec(b) for b in rights],
        out_specs=pl.BlockSpec((block, width), lambda i: (i, 0)),
        compiler_params=pltpu.CompilerParams(
            dimension_semantics=("arbitrary",), vmem_limit_bytes=VMEM_BYTES
        ),
        cost_estimate=pl.CostEstimate(
            flops=2 * parts * rows * height * width // shrink,
            bytes_accessed=2 * (parts * rows * (height + width) + height * width) // shrink,
            transcendentals=0,
        ),
        name="outer",
    )(*lefts, *rights)


def finish(pieces, weights, gain, moves):
    count, rows = len(weights), gain.shape[0]

    def body(*refs):
        pieces_ref, gain_ref, weight_refs = refs[0], refs[1], refs[2 : 2 + count]
        outs, total_ref = refs[2 + count : -1], refs[-1]
        scale = gain_ref[...]
        total = jnp.zeros((rows, HD), F32)
        for sender, source, which, target in moves:
            value = pieces_ref[sender, :, source].astype(F32)
            outs[which][:, target] = value * scale
            product = value * weight_refs[which][:, target].astype(F32)
            for at in tiles(product.shape[1], HD):
                total += product[:, at]
        total_ref[...] = jnp.broadcast_to(jnp.sum(total, axis=1, keepdims=True), (rows, HD))

    out = pl.pallas_call(
        body,
        out_shape=[jax.ShapeDtypeStruct(w.shape, F32) for w in weights]
        + [jax.ShapeDtypeStruct((rows, HD), F32)],
        cost_estimate=pl.CostEstimate(
            flops=pieces.size // SHRINK, bytes_accessed=pieces.size // SHRINK, transcendentals=0
        ),
        compiler_params=pltpu.CompilerParams(vmem_limit_bytes=VMEM_BYTES),
        name="finish",
    )(pieces, gain, *weights)
    return out[:-1], out[-1][:, 0]


def after(value, *earlier):
    return lax.optimization_barrier((value,) + earlier)[0]


def swap(value, mask):
    count = lax.axis_size("dp") * lax.axis_size("fsdp")
    return lax.ppermute(value, BOTH, [(i, i ^ mask) for i in range(count)])


def add_low(left, right):
    return (left.astype(F32) + right.astype(F32)).astype(BF16)


def is_paired():
    return lax.axis_size("dp") == 4 and lax.axis_size("fsdp") == 8


def order_of(first, second):
    return ((0, first, second, first | second), (0, second, first, first | second))


def gather_group(rows, first, second, *meanwhile):
    if not is_paired():
        whole = lax.all_gather(rows, "fsdp", axis=1)
        return [whole.reshape(-1, rows.shape[-1])]
    a, b = rows[0], rows[1]
    a1, b2 = swap(a, first), swap(b, second)
    a2, b1 = swap(a, second), swap(b, first)
    a3, b3 = swap(a1, second), swap(b2, first)
    own = jnp.concatenate([a, a1, a2, a3, b, b2, b1, b3], axis=0)
    return [own, swap(after(own, *meanwhile) if meanwhile else own, CORE)]


def scatter_group(parts, first, second, like, fill=None, late=None):
    if not is_paired():
        micro, length, width = like.shape
        blocks = parts[0].reshape(micro, -1, length, width)
        if fill is not None:
            fill(lambda value: value)
        if late is not None:
            late(lambda value: value)
        return lax.psum_scatter(blocks, "fsdp", scatter_dimension=1).astype(F32)
    keep, send = (part.reshape((2, 4) + like.shape[1:]) for part in parts)
    got = swap(send, CORE)
    a, a_far = add_low(keep[0, :2], got[0, :2]), add_low(keep[0, 2:], got[0, 2:])
    b, b_far = add_low(keep[1, :2], got[1, :2]), add_low(keep[1, 2:], got[1, 2:])
    if fill is not None:
        fill(lambda value: after(value, a_far, b_far))
    a_got, b_got = swap(a_far, second), swap(b_far, first)
    if late is not None:
        late(lambda value: after(value, a_got, b_got))
    a, a_far = add_low(a[0], a_got[0]), add_low(a[1], a_got[1])
    b, b_far = add_low(b[0], b_got[0]), add_low(b[1], b_got[1])
    a_got, b_got = swap(a_far, first), swap(b_far, second)
    return jnp.stack([a.astype(F32) + a_got.astype(F32), b.astype(F32) + b_got.astype(F32)])


def per_device(
    tokens,
    lengths,
    order,
    w_query,
    w_key,
    w_value,
    w_output,
    w_gate,
    w_up,
    w_down,
    gain_attn,
    gain_ffn,
    cotangent,
):
    groups, members = lax.axis_size("dp"), lax.axis_size("fsdp")
    plane, member = lax.axis_index("dp"), lax.axis_index("fsdp")
    paired = is_paired()
    micro, _, cap, width = tokens.shape
    own_rows = w_query.shape[0]
    hidden = w_gate.shape[1]
    share = hidden // members
    sharers = HD // own_rows
    kinds = members // sharers
    my_heads = groups // sharers
    head_cols = my_heads * HD

    slots = jnp.arange(order.shape[1], dtype=jnp.int32)
    me = plane * members + member
    position = jnp.arange(cap, dtype=jnp.int32)

    if paired:
        block = jnp.array(
            [mask | core for core in (0, CORE) for masks in order_of(X, Y) for mask in masks]
        )
        devices = (me ^ block).reshape(2, 2, 4)
    else:
        devices = jnp.broadcast_to(plane * members + jnp.arange(members), (1, micro, members))
    placed = jnp.sum(
        jnp.where(devices[..., None] == slots, order[None, :, None, :], 0), axis=-1
    )
    lives = jnp.sum(
        jnp.where(placed[..., None] == slots, lengths[None, :, None, :], 0), axis=-1
    ).reshape(-1)

    my_slot = jnp.sum(jnp.where(slots == me, order, 0), axis=-1)
    my_live = jnp.sum(jnp.where(slots == my_slot[:, None], lengths, 0), axis=-1)
    my_mask = (position < my_live[:, None]).astype(F32)[:, :, None]

    gain_one = gain_attn.astype(F32)[:, None]
    gain_two = gain_ffn.astype(F32)[:, None]

    def scaled(weight, gain):
        return (weight.astype(F32) * gain).astype(BF16)

    def by_head(weight):
        cut = weight.reshape(own_rows, sharers, my_heads, kinds, HD)
        return cut.transpose(3, 1, 0, 2, 4).reshape(members, own_rows, head_cols)

    def by_unit(weight):
        return weight.reshape(own_rows, members, share).transpose(1, 0, 2)

    def planes(value):
        return lax.all_gather(value, "dp", axis=0, tiled=True)

    def over_planes(value):
        return lax.psum_scatter(value, "dp", scatter_dimension=0, tiled=True)

    def spread(pieces):
        count, rows, columns = pieces.shape
        flat = pieces.reshape(count * rows, columns)
        return lax.all_to_all(flat, "fsdp", 0, 0, tiled=True)

    cut_qkv = jnp.concatenate(
        [by_head(scaled(w, gain_one)) for w in (w_query, w_key, w_value)], axis=2
    )
    cut_gu = jnp.concatenate([by_unit(scaled(w, gain_two)) for w in (w_gate, w_up)], axis=2)
    cut_d = by_unit(w_down)
    near_qkv = spread(cut_qkv)
    wqkv = planes(near_qkv)
    raw = planes(w_output).reshape(sharers, my_heads, own_rows, width)
    subgroups = [[s * sharers + i for i in range(sharers)] for s in range(kinds)]

    def exchange(value):
        if not paired:
            return lax.all_to_all(value, "fsdp", 0, 0, axis_index_groups=subgroups)
        odd = (member & CORE) != 0
        mine, send = jnp.where(odd, value[1], value[0]), jnp.where(odd, value[0], value[1])
        got = swap(send, CORE)
        return jnp.stack([jnp.where(odd, got, mine), jnp.where(odd, mine, got)])

    wo = exchange(raw).transpose(1, 0, 2, 3).reshape(head_cols, width)

    x = after(tokens, near_qkv)[:, 0].astype(F32)
    inverse_one = lax.rsqrt(jnp.mean(x * x, axis=-1, keepdims=True) + EPSILON)
    normal_one = x * inverse_one
    n1 = gather_group(normal_one.astype(BF16), X, Y)
    near_gu = spread(after(cut_gu, near_qkv))
    upstream = cotangent[:, 0].astype(F32) * my_mask
    returned_grad = gather_group(after(upstream.astype(BF16), n1[0], near_gu), X, Y)
    near_d = spread(after(cut_d, returned_grad[0]))
    wgu, wd = planes(near_gu), planes(near_d)
    n1[0] = after(n1[0], near_gu)

    cosine, sine = rope_tables(cap, ROWS // cap)
    parts, qkv, mixed = attention_forward(n1, lives, wqkv, wo, cosine, sine, cap)
    parts = [*parts[:-1], after(parts[-1], *returned_grad)]
    attended = scatter_group(parts, X, Y, x)
    hidden_one = x + attended

    inverse_two = lax.rsqrt(jnp.mean(hidden_one * hidden_one, axis=-1, keepdims=True) + EPSILON)
    normal_two = hidden_one * inverse_two
    n2 = gather_group(normal_two.astype(BF16), X, Y, wgu)
    gate, up, activated = feed_forward(n2, wgu)

    part_d = outer(returned_grad, [activated], ROWS)
    returned_grad = list(lax.optimization_barrier((*returned_grad, part_d))[:-1])
    sum_d = over_planes(part_d)
    parts, grad_gu = feed_back(returned_grad, gate, up, wd, wgu)
    travelling = {}

    def fill(tie):
        travelling["gu"] = outer([tie(n2[0]), *n2[1:]], [grad_gu], ROWS, 1)

    back_two = after(scatter_group(parts, X, Y, x, fill), travelling["gu"], sum_d)
    sum_gu = over_planes(travelling["gu"])
    grad_hidden = upstream + inverse_two * (
        back_two - normal_two * jnp.mean(back_two * normal_two, axis=-1, keepdims=True)
    )
    grad_low = grad_hidden.astype(BF16)
    def home(mine):
        return lax.all_to_all(mine, "fsdp", 0, 0, tiled=True).reshape(members, own_rows, -1)

    grad_attended = gather_group(grad_low, X, Y)
    part_o = outer([mixed], grad_attended, HD)
    grad_attended = [after(grad_attended[0], part_o), *grad_attended[1:]]
    parts, grad_qkv = attention_backward(grad_attended, lives, qkv, wqkv, wo, cosine, sine, cap)
    part_o = exchange(part_o.reshape(my_heads, sharers, own_rows, width).transpose(1, 0, 2, 3))
    part_qkv = outer(n1, [grad_qkv], ROWS, 1)
    grad_wo = over_planes(after(part_o.reshape(groups * own_rows, width), sum_gu, part_qkv))
    sum_qkv = over_planes(after(part_qkv, sum_gu))
    ties = []
    homes = []

    def go_home(tie):
        homes.append(home(jnp.concatenate([sum_d, tie(sum_gu)], axis=1)))

    back_one = scatter_group(parts, X, Y, x, ties.append, go_home)
    parts = feed_down(ties[0](after(activated, part_qkv)), wd, len(n2))
    returned = scatter_group(parts, X, Y, x)
    back_one, sum_dgu, returned, sum_qkv = lax.optimization_barrier(
        (back_one, homes[0], returned, sum_qkv)
    )
    output = ((hidden_one + returned) * my_mask).astype(BF16)
    sum_d, sum_gu = sum_dgu[:, :, :share], sum_dgu[:, :, share:]
    grad_tokens = (
        grad_hidden
        + inverse_one
        * (back_one - normal_one * jnp.mean(back_one * normal_one, axis=-1, keepdims=True))
    ).astype(BF16)

    sum_qkv = home(sum_qkv)

    def from_units(value):
        return value.transpose(1, 0, 2).reshape(own_rows, hidden).astype(F32)

    moves_qkv = [
        (
            p * sharers + c,
            slice(kind * head_cols + m * HD, kind * head_cols + (m + 1) * HD),
            kind,
            slice(((c * my_heads + m) * kinds + p) * HD, ((c * my_heads + m) * kinds + p + 1) * HD),
        )
        for kind in range(3)
        for p in range(kinds)
        for c in range(sharers)
        for m in range(my_heads)
    ]
    grad_qkv, grad_gain_one = finish(sum_qkv, (w_query, w_key, w_value), gain_one, moves_qkv)
    raw_gu = [from_units(sum_gu[:, :, i * share : (i + 1) * share]) for i in range(2)]
    grad_gain_two = sum(
        jnp.sum(g * w.astype(F32), axis=1) for g, w in zip(raw_gu, (w_gate, w_up), strict=True)
    )
    return (
        output[:, None],
        grad_tokens[:, None],
        *grad_qkv,
        grad_wo.astype(F32),
        raw_gu[0] * gain_two,
        raw_gu[1] * gain_two,
        from_units(sum_d),
        grad_gain_one,
        grad_gain_two,
    )


def solution(mesh):
    sequences = P(None, BOTH, None, None)
    rows = P(BOTH, None)
    in_specs = (sequences, P(), P()) + (rows,) * 7 + (P(BOTH), P(BOTH), sequences)
    out_specs = (sequences, sequences) + (rows,) * 7 + (P(BOTH), P(BOTH))
    return jax.shard_map(
        per_device, mesh=mesh, in_specs=in_specs, out_specs=out_specs, check_vma=False
    )
```

```python
import math

import jax
import jax.numpy as jnp
from jax import lax
from jax.experimental import pallas as pl
from jax.experimental.pallas import tpu as pltpu
from jax.sharding import PartitionSpec as P

H = 16
HD = 128
EPSILON = 1e-05
F32 = jnp.float32
BF16 = jnp.bfloat16
BOTH = ("dp", "fsdp")
CORE, X, Y = 1, 2, 4
ROWS = 512
SHRINK = 50
VMEM_BYTES = 60 * 1024 * 1024


def rope_tables(length_cap, repeats):
    halfway = HD // 2
    position = jnp.arange(length_cap, dtype=F32)
    inverse = 10000.0 ** (-2.0 * jnp.arange(halfway, dtype=F32) / HD)
    angles = position[:, None] * inverse[None, :]
    cosine, sine = jnp.cos(angles), jnp.sin(angles)
    cosine = jnp.concatenate([cosine, cosine], axis=1)
    sine = jnp.concatenate([-sine, sine], axis=1)
    return jnp.tile(cosine, (repeats, 1)), jnp.tile(sine, (repeats, 1))


def dot_nn(left, right):
    return lax.dot_general(left, right, (((1,), (0,)), ((), ())), preferred_element_type=F32)


def dot_nt(left, right):
    return lax.dot_general(left, right, (((1,), (1,)), ((), ())), preferred_element_type=F32)


def dot_tn(left, right):
    return lax.dot_general(left, right, (((0,), (0,)), ((), ())), preferred_element_type=F32)


def whole_spec(array):
    return pl.BlockSpec(array.shape, lambda i, *_: (0,) * array.ndim, pipeline_mode=pl.Buffered(1))


def part_specs(count, steps, columns):
    def spec(k):
        return pl.BlockSpec(
            (ROWS, columns), lambda i, *_: (jnp.clip(i - k * steps, 0, steps - 1), 0)
        )

    return [spec(k) for k in range(count)]


def row_spec(columns):
    return pl.BlockSpec((ROWS, columns), lambda i, *_: (i, 0))


def by_part(count, steps, work):
    if count == 1:
        work(0)
        return
    for k in range(count):
        pl.when(pl.program_id(0) // steps == k)(lambda k=k: work(k))


def tiles(extent, size):
    size = min(size, extent)
    return [slice(at, at + size) for at in range(0, extent, size)]


def call(body, name, parts, rows, whole, scalars, part_outs, row_outs, flops, scratch=(), shrink=SHRINK):
    count = len(parts)
    steps = parts[0].shape[0] // ROWS if parts else rows[0].shape[0] // ROWS
    cuts = count if parts else 1
    total = steps * max(cuts, 1)
    out_shape, out_specs = [], []
    for columns, dtype, pieces in part_outs:
        per = total // pieces
        out_shape += [jax.ShapeDtypeStruct((per * ROWS, columns), dtype)] * pieces
        out_specs += part_specs(pieces, per, columns)
    for columns, dtype in row_outs:
        out_shape.append(jax.ShapeDtypeStruct((total * ROWS, columns), dtype))
        out_specs.append(row_spec(columns))
    in_specs = part_specs(count, steps, parts[0].shape[1]) if parts else []
    in_specs += [row_spec(r.shape[1]) for r in rows] + [whole_spec(w) for w in whole]
    moved = sum(a.size * a.dtype.itemsize for a in list(parts) + list(rows) + list(whole))
    moved += sum(math.prod(o.shape) * jnp.dtype(o.dtype).itemsize for o in out_shape)
    return pl.pallas_call(
        body,
        out_shape=out_shape,
        grid_spec=pltpu.PrefetchScalarGridSpec(
            num_scalar_prefetch=len(scalars), grid=(total,), in_specs=in_specs, out_specs=out_specs,
            scratch_shapes=list(scratch),
        ),
        compiler_params=pltpu.CompilerParams(
            dimension_semantics=("arbitrary",), vmem_limit_bytes=VMEM_BYTES
        ),
        cost_estimate=pl.CostEstimate(flops=flops // shrink, bytes_accessed=moved // shrink, transcendentals=0),
        name=name,
    )(*scalars, *parts, *rows, *whole)


def turn(value, cosine, sine):
    return value * cosine + pltpu.roll(value, HD // 2, 1) * sine


def allowed_of(live, cap):
    row = lax.broadcasted_iota(jnp.int32, (cap, cap), 0)
    column = lax.broadcasted_iota(jnp.int32, (cap, cap), 1)
    return (row >= column) & (column < live)


def attention_forward(parts, live, wqkv, wo, cosine, sine, cap):
    count, cols, width = len(parts), wo.shape[0], wo.shape[1]
    steps = parts[0].shape[0] // ROWS
    scale, shift = 1.0 / math.sqrt(HD), -math.log(cap)

    def body(live_ref, *refs):
        sources, refs = refs[:count], refs[count:]
        wqkv_ref, wo_ref, cos_ref, sin_ref = refs[:4]
        outs, (qkv_ref, mixed_ref) = refs[4 : 4 + count], refs[4 + count :]
        step = pl.program_id(0)

        def project(part):
            rows = sources[part][...]
            for kind in range(3):
                value = dot_nn(rows, wqkv_ref[:, kind * cols : (kind + 1) * cols])
                for head in tiles(cols, HD):
                    one = value[:, head]
                    if kind < 2:
                        one = turn(one, cos_ref[...], sin_ref[...])
                    at = slice(kind * cols + head.start, kind * cols + head.stop)
                    qkv_ref[:, at] = one.astype(BF16)

        by_part(count, steps, project)
        for k, sequence in enumerate(tiles(ROWS, cap)):
            allowed = allowed_of(live_ref[step * (ROWS // cap) + k], cap)
            for head in tiles(cols, HD):
                query = qkv_ref[sequence, head]
                key = qkv_ref[sequence, cols + head.start : cols + head.stop]
                value = qkv_ref[sequence, 2 * cols + head.start : 2 * cols + head.stop]
                gates = jax.nn.sigmoid(dot_nt(query, key) * scale + shift)
                probs = jnp.where(allowed, gates, 0.0).astype(BF16)
                mixed_ref[sequence, head] = dot_nn(probs, value).astype(BF16)

        def finish(part):
            outs[part][...] = dot_nn(mixed_ref[...], wo_ref[...]).astype(BF16)

        by_part(count, steps, finish)

    total = count * steps * ROWS
    out = call(
        body,
        "attention_forward",
        parts,
        [],
        [wqkv, wo, cosine, sine],
        [live],
        [(width, BF16, count)],
        [(3 * cols, BF16), (cols, BF16)],
        2 * total * width * 4 * cols,
    )
    return out[:count], out[count], out[count + 1]


def attention_backward(parts, live, qkv, wqkv, wo, cosine, sine, cap):
    count, cols, width = len(parts), wo.shape[0], wo.shape[1]
    steps = parts[0].shape[0] // ROWS
    scale, shift = 1.0 / math.sqrt(HD), -math.log(cap)

    def body(live_ref, *refs):
        sources, refs = refs[:count], refs[count:]
        qkv_ref, wqkv_ref, wo_ref, cos_ref, sin_ref = refs[:5]
        outs, (back_ref, mixed_ref) = refs[5 : 5 + count], refs[5 + count :]
        step = pl.program_id(0)

        def enter(part):
            mixed_ref[...] = dot_nt(sources[part][...], wo_ref[...]).astype(BF16)

        by_part(count, steps, enter)
        for k, sequence in enumerate(tiles(ROWS, cap)):
            allowed = allowed_of(live_ref[step * (ROWS // cap) + k], cap)
            cosine_here, sine_here = cos_ref[sequence, :], sin_ref[sequence, :]
            for head in tiles(cols, HD):
                key_at = slice(cols + head.start, cols + head.stop)
                value_at = slice(2 * cols + head.start, 2 * cols + head.stop)
                query, key, value = (
                    qkv_ref[sequence, at] for at in (head, key_at, value_at)
                )
                grad = mixed_ref[sequence, head]
                gates = jax.nn.sigmoid(dot_nt(query, key) * scale + shift)
                probs = jnp.where(allowed, gates, 0.0).astype(BF16)
                grad_logits = dot_nt(grad, value) * gates * (1.0 - gates)
                grad_logits = jnp.where(allowed, grad_logits, 0.0).astype(BF16)
                grad_query = dot_nn(grad_logits, key) * scale
                grad_key = dot_tn(grad_logits, query) * scale
                back_ref[sequence, head] = turn(grad_query, cosine_here, -sine_here).astype(BF16)
                back_ref[sequence, key_at] = turn(grad_key, cosine_here, -sine_here).astype(BF16)
                back_ref[sequence, value_at] = dot_tn(probs, grad).astype(BF16)

        def finish(part):
            outs[part][...] = dot_nt(back_ref[...], wqkv_ref[...]).astype(BF16)

        by_part(count, steps, finish)

    total = count * steps * ROWS
    out = call(
        body,
        "attention_backward",
        parts,
        [qkv],
        [wqkv, wo, cosine, sine],
        [live],
        [(width, BF16, count)],
        [(3 * cols, BF16)],
        2 * total * width * 4 * cols,
        [pltpu.VMEM((ROWS, cols), BF16)],
        1,
    )
    return out[:count], out[count]


def feed_forward(parts, wgu):
    count, width = len(parts), wgu.shape[0]
    share = wgu.shape[1] // 2
    steps = parts[0].shape[0] // ROWS

    def body(*refs):
        sources, (wgu_ref, gate_ref, up_ref, active_ref) = refs[:count], refs[count:]

        def work(part):
            rows = sources[part][...]
            for at in tiles(share, 256):
                gate = dot_nn(rows, wgu_ref[:, at])
                up = dot_nn(rows, wgu_ref[:, share + at.start : share + at.stop])
                gate_ref[:, at] = gate
                up_ref[:, at] = up
                active_ref[:, at] = (gate * jax.nn.sigmoid(gate) * up).astype(BF16)

        by_part(count, steps, work)

    total = count * steps * ROWS
    return call(
        body,
        "feed_forward",
        parts,
        [],
        [wgu],
        [],
        [],
        [(share, F32), (share, F32), (share, BF16)],
        4 * total * width * share,
    )


def feed_back(parts, gate, up, wd, wgu):
    count, width = len(parts), wgu.shape[0]
    share = wgu.shape[1] // 2
    steps = parts[0].shape[0] // ROWS

    def body(*refs):
        sources, refs = refs[:count], refs[count:]
        gate_ref, up_ref, wd_ref, wgu_ref = refs[:4]
        outs, (grad_ref,) = refs[4 : 4 + count], refs[4 + count :]

        def work(part):
            rows = sources[part][...]
            for at in tiles(share, 256):
                grad = dot_nn(rows, wd_ref[:, at])
                gate = gate_ref[:, at]
                open_gate = jax.nn.sigmoid(gate)
                grad_gate = grad * up_ref[:, at] * (open_gate * (1.0 + gate * (1.0 - open_gate)))
                grad_ref[:, at] = grad_gate.astype(BF16)
                grad_up = grad * (gate * open_gate)
                grad_ref[:, share + at.start : share + at.stop] = grad_up.astype(BF16)
            grads = grad_ref[...]
            for at in tiles(width, 512):
                outs[part][:, at] = dot_nt(grads, wgu_ref[at, :]).astype(BF16)

        by_part(count, steps, work)

    total = count * steps * ROWS
    out = call(
        body,
        "feed_back",
        parts,
        [gate, up],
        [wd, wgu],
        [],
        [(width, BF16, count)],
        [(2 * share, BF16)],
        6 * total * width * share,
    )
    return out[:count], out[count]


def feed_down(active, wd, pieces):
    width = wd.shape[0]
    steps = active.shape[0] // ROWS // pieces

    def body(active_ref, wd_ref, *outs):
        def work(part):
            rows = active_ref[...]
            for at in tiles(width, 512):
                outs[part][:, at] = dot_nt(rows, wd_ref[at, :]).astype(BF16)

        by_part(pieces, steps, work)

    return call(
        body,
        "feed_down",
        [],
        [active],
        [wd],
        [],
        [(width, BF16, pieces)],
        [],
        2 * active.size * width,
        shrink=1,
    )


def outer(lefts, rights, block, shrink=SHRINK):
    parts = max(len(lefts), len(rights))
    rows = lefts[0].shape[0] * len(lefts) // parts
    height, width = lefts[0].shape[1], rights[0].shape[1]
    nleft = len(lefts)

    def body(*refs):
        def pieces(group):
            if len(group) == parts:
                return [ref[...] for ref in group]
            return [group[0][k * rows : (k + 1) * rows, :] for k in range(parts)]

        left, right = pieces(refs[:nleft]), pieces(refs[nleft:-1])
        total = dot_tn(left[0], right[0])
        for one, other in zip(left[1:], right[1:], strict=True):
            total += dot_tn(one, other)
        refs[-1][...] = total.astype(BF16)

    return pl.pallas_call(
        body,
        out_shape=jax.ShapeDtypeStruct((height, width), BF16),
        grid=(height // block,),
        in_specs=[pl.BlockSpec((a.shape[0], block), lambda i: (0, i)) for a in lefts]
        + [whole_spec(b) for b in rights],
        out_specs=pl.BlockSpec((block, width), lambda i: (i, 0)),
        compiler_params=pltpu.CompilerParams(
            dimension_semantics=("arbitrary",), vmem_limit_bytes=VMEM_BYTES
        ),
        cost_estimate=pl.CostEstimate(
            flops=2 * parts * rows * height * width // shrink,
            bytes_accessed=2 * (parts * rows * (height + width) + height * width) // shrink,
            transcendentals=0,
        ),
        name="outer",
    )(*lefts, *rights)


def finish(pieces, weights, gain, moves):
    count, rows = len(weights), gain.shape[0]

    def body(*refs):
        pieces_ref, gain_ref, weight_refs = refs[0], refs[1], refs[2 : 2 + count]
        outs, total_ref = refs[2 + count : -1], refs[-1]
        scale = gain_ref[...]
        total = jnp.zeros((rows, HD), F32)
        for sender, source, which, target in moves:
            value = pieces_ref[sender, :, source].astype(F32)
            outs[which][:, target] = value * scale
            product = value * weight_refs[which][:, target].astype(F32)
            for at in tiles(product.shape[1], HD):
                total += product[:, at]
        total_ref[...] = jnp.broadcast_to(jnp.sum(total, axis=1, keepdims=True), (rows, HD))

    out = pl.pallas_call(
        body,
        out_shape=[jax.ShapeDtypeStruct(w.shape, F32) for w in weights]
        + [jax.ShapeDtypeStruct((rows, HD), F32)],
        cost_estimate=pl.CostEstimate(
            flops=pieces.size // SHRINK, bytes_accessed=pieces.size // SHRINK, transcendentals=0
        ),
        compiler_params=pltpu.CompilerParams(vmem_limit_bytes=VMEM_BYTES),
        name="finish",
    )(pieces, gain, *weights)
    return out[:-1], out[-1][:, 0]


def after(value, *earlier):
    return lax.optimization_barrier((value,) + earlier)[0]


def swap(value, mask):
    count = lax.axis_size("dp") * lax.axis_size("fsdp")
    return lax.ppermute(value, BOTH, [(i, i ^ mask) for i in range(count)])


def add_low(left, right):
    return (left.astype(F32) + right.astype(F32)).astype(BF16)


def is_paired():
    return lax.axis_size("dp") == 4 and lax.axis_size("fsdp") == 8


def order_of(first, second):
    return ((0, first, second, first | second), (0, second, first, first | second))


def gather_group(rows, first, second, *meanwhile):
    if not is_paired():
        whole = lax.all_gather(rows, "fsdp", axis=1)
        return [whole.reshape(-1, rows.shape[-1])]
    a, b = rows[0], rows[1]
    a1, b2 = swap(a, first), swap(b, second)
    a2, b1 = swap(a, second), swap(b, first)
    a3, b3 = swap(a1, second), swap(b2, first)
    own = jnp.concatenate([a, a1, a2, a3, b, b2, b1, b3], axis=0)
    return [own, swap(after(own, *meanwhile) if meanwhile else own, CORE)]


def scatter_group(parts, first, second, like, fill=None, late=None):
    if not is_paired():
        micro, length, width = like.shape
        blocks = parts[0].reshape(micro, -1, length, width)
        if fill is not None:
            fill(lambda value: value)
        if late is not None:
            late(lambda value: value)
        return lax.psum_scatter(blocks, "fsdp", scatter_dimension=1).astype(F32)
    keep, send = (part.reshape((2, 4) + like.shape[1:]) for part in parts)
    got = swap(send, CORE)
    a, a_far = add_low(keep[0, :2], got[0, :2]), add_low(keep[0, 2:], got[0, 2:])
    b, b_far = add_low(keep[1, :2], got[1, :2]), add_low(keep[1, 2:], got[1, 2:])
    if fill is not None:
        fill(lambda value: after(value, a_far, b_far))
    a_got, b_got = swap(a_far, second), swap(b_far, first)
    if late is not None:
        late(lambda value: after(value, a_got, b_got))
    a, a_far = add_low(a[0], a_got[0]), add_low(a[1], a_got[1])
    b, b_far = add_low(b[0], b_got[0]), add_low(b[1], b_got[1])
    a_got, b_got = swap(a_far, first), swap(b_far, second)
    return jnp.stack([a.astype(F32) + a_got.astype(F32), b.astype(F32) + b_got.astype(F32)])


def per_device(
    tokens,
    lengths,
    order,
    w_query,
    w_key,
    w_value,
    w_output,
    w_gate,
    w_up,
    w_down,
    gain_attn,
    gain_ffn,
    cotangent,
):
    groups, members = lax.axis_size("dp"), lax.axis_size("fsdp")
    plane, member = lax.axis_index("dp"), lax.axis_index("fsdp")
    paired = is_paired()
    micro, _, cap, width = tokens.shape
    own_rows = w_query.shape[0]
    hidden = w_gate.shape[1]
    share = hidden // members
    sharers = HD // own_rows
    kinds = members // sharers
    my_heads = groups // sharers
    head_cols = my_heads * HD

    slots = jnp.arange(order.shape[1], dtype=jnp.int32)
    me = plane * members + member
    position = jnp.arange(cap, dtype=jnp.int32)

    if paired:
        block = jnp.array(
            [mask | core for core in (0, CORE) for masks in order_of(X, Y) for mask in masks]
        )
        devices = (me ^ block).reshape(2, 2, 4)
    else:
        devices = jnp.broadcast_to(plane * members + jnp.arange(members), (1, micro, members))
    placed = jnp.sum(
        jnp.where(devices[..., None] == slots, order[None, :, None, :], 0), axis=-1
    )
    lives = jnp.sum(
        jnp.where(placed[..., None] == slots, lengths[None, :, None, :], 0), axis=-1
    ).reshape(-1)

    my_slot = jnp.sum(jnp.where(slots == me, order, 0), axis=-1)
    my_live = jnp.sum(jnp.where(slots == my_slot[:, None], lengths, 0), axis=-1)
    my_mask = (position < my_live[:, None]).astype(F32)[:, :, None]

    gain_one = gain_attn.astype(F32)[:, None]
    gain_two = gain_ffn.astype(F32)[:, None]

    def scaled(weight, gain):
        return (weight.astype(F32) * gain).astype(BF16)

    def by_head(weight):
        cut = weight.reshape(own_rows, sharers, my_heads, kinds, HD)
        return cut.transpose(3, 1, 0, 2, 4).reshape(members, own_rows, head_cols)

    def by_unit(weight):
        return weight.reshape(own_rows, members, share).transpose(1, 0, 2)

    def planes(value):
        return lax.all_gather(value, "dp", axis=0, tiled=True)

    def over_planes(value):
        return lax.psum_scatter(value, "dp", scatter_dimension=0, tiled=True)

    def spread(pieces):
        count, rows, columns = pieces.shape
        flat = pieces.reshape(count * rows, columns)
        return lax.all_to_all(flat, "fsdp", 0, 0, tiled=True)

    cut_qkv = jnp.concatenate(
        [by_head(scaled(w, gain_one)) for w in (w_query, w_key, w_value)], axis=2
    )
    cut_gu = jnp.concatenate([by_unit(scaled(w, gain_two)) for w in (w_gate, w_up)], axis=2)
    cut_d = by_unit(w_down)
    near_qkv = spread(cut_qkv)
    wqkv = planes(near_qkv)
    raw = planes(w_output).reshape(sharers, my_heads, own_rows, width)
    subgroups = [[s * sharers + i for i in range(sharers)] for s in range(kinds)]

    def exchange(value):
        if not paired:
            return lax.all_to_all(value, "fsdp", 0, 0, axis_index_groups=subgroups)
        odd = (member & CORE) != 0
        mine, send = jnp.where(odd, value[1], value[0]), jnp.where(odd, value[0], value[1])
        got = swap(send, CORE)
        return jnp.stack([jnp.where(odd, got, mine), jnp.where(odd, mine, got)])

    wo = exchange(raw).transpose(1, 0, 2, 3).reshape(head_cols, width)

    x = after(tokens, near_qkv)[:, 0].astype(F32)
    inverse_one = lax.rsqrt(jnp.mean(x * x, axis=-1, keepdims=True) + EPSILON)
    normal_one = x * inverse_one
    n1 = gather_group(normal_one.astype(BF16), X, Y)
    near_gu = spread(after(cut_gu, near_qkv))
    upstream = cotangent[:, 0].astype(F32) * my_mask
    returned_grad = gather_group(after(upstream.astype(BF16), n1[0], near_gu), X, Y)
    near_d = spread(after(cut_d, returned_grad[0]))
    wgu, wd = planes(near_gu), planes(near_d)
    n1[0] = after(n1[0], near_gu)

    cosine, sine = rope_tables(cap, ROWS // cap)
    parts, qkv, mixed = attention_forward(n1, lives, wqkv, wo, cosine, sine, cap)
    parts = [*parts[:-1], after(parts[-1], *returned_grad)]
    attended = scatter_group(parts, X, Y, x)
    hidden_one = x + attended

    inverse_two = lax.rsqrt(jnp.mean(hidden_one * hidden_one, axis=-1, keepdims=True) + EPSILON)
    normal_two = hidden_one * inverse_two
    n2 = gather_group(normal_two.astype(BF16), X, Y, wgu)
    gate, up, activated = feed_forward(n2, wgu)

    part_d = outer(returned_grad, [activated], ROWS)
    returned_grad = list(lax.optimization_barrier((*returned_grad, part_d))[:-1])
    sum_d = over_planes(part_d)
    parts, grad_gu = feed_back(returned_grad, gate, up, wd, wgu)
    travelling = {}

    def fill(tie):
        travelling["gu"] = outer([tie(n2[0]), *n2[1:]], [grad_gu], ROWS, 1)

    back_two = after(scatter_group(parts, X, Y, x, fill), travelling["gu"], sum_d)
    sum_gu = over_planes(travelling["gu"])
    grad_hidden = upstream + inverse_two * (
        back_two - normal_two * jnp.mean(back_two * normal_two, axis=-1, keepdims=True)
    )
    grad_low = grad_hidden.astype(BF16)
    def home(mine):
        return lax.all_to_all(mine, "fsdp", 0, 0, tiled=True).reshape(members, own_rows, -1)

    grad_attended = gather_group(grad_low, X, Y)
    part_o = outer([mixed], grad_attended, HD)
    grad_attended = [after(grad_attended[0], part_o), *grad_attended[1:]]
    parts, grad_qkv = attention_backward(grad_attended, lives, qkv, wqkv, wo, cosine, sine, cap)
    part_o = exchange(part_o.reshape(my_heads, sharers, own_rows, width).transpose(1, 0, 2, 3))
    part_qkv = outer(n1, [grad_qkv], ROWS, 1)
    grad_wo = over_planes(after(part_o.reshape(groups * own_rows, width), sum_gu, part_qkv))
    sum_qkv = over_planes(after(part_qkv, sum_gu))
    ties = []
    homes = []

    def go_home(tie):
        homes.append(home(jnp.concatenate([sum_d, tie(sum_gu)], axis=1)))

    back_one = scatter_group(parts, X, Y, x, ties.append, go_home)
    parts = feed_down(ties[0](after(activated, part_qkv)), wd, len(n2))
    returned = scatter_group(parts, X, Y, x)
    sum_dgu, sum_qkv = lax.optimization_barrier((homes[0], sum_qkv))
    output = ((hidden_one + returned) * my_mask).astype(BF16)
    sum_d, sum_gu = sum_dgu[:, :, :share], sum_dgu[:, :, share:]
    grad_tokens = (
        grad_hidden
        + inverse_one
        * (back_one - normal_one * jnp.mean(back_one * normal_one, axis=-1, keepdims=True))
    ).astype(BF16)

    sum_qkv = home(sum_qkv)

    def from_units(value):
        return value.transpose(1, 0, 2).reshape(own_rows, hidden).astype(F32)

    moves_qkv = [
        (
            p * sharers + c,
            slice(kind * head_cols + m * HD, kind * head_cols + (m + 1) * HD),
            kind,
            slice(((c * my_heads + m) * kinds + p) * HD, ((c * my_heads + m) * kinds + p + 1) * HD),
        )
        for kind in range(3)
        for p in range(kinds)
        for c in range(sharers)
        for m in range(my_heads)
    ]
    grad_qkv, grad_gain_one = finish(sum_qkv, (w_query, w_key, w_value), gain_one, moves_qkv)
    raw_gu = [from_units(sum_gu[:, :, i * share : (i + 1) * share]) for i in range(2)]
    grad_gain_two = sum(
        jnp.sum(g * w.astype(F32), axis=1) for g, w in zip(raw_gu, (w_gate, w_up), strict=True)
    )
    return (
        output[:, None],
        grad_tokens[:, None],
        *grad_qkv,
        grad_wo.astype(F32),
        raw_gu[0] * gain_two,
        raw_gu[1] * gain_two,
        from_units(sum_d),
        grad_gain_one,
        grad_gain_two,
    )


def solution(mesh):
    sequences = P(None, BOTH, None, None)
    rows = P(BOTH, None)
    in_specs = (sequences, P(), P()) + (rows,) * 7 + (P(BOTH), P(BOTH), sequences)
    out_specs = (sequences, sequences) + (rows,) * 7 + (P(BOTH), P(BOTH))
    return jax.shard_map(
        per_device, mesh=mesh, in_specs=in_specs, out_specs=out_specs, check_vma=False
    )
```
